128 devices in a mesh: req: 16 (over y, z), mlp: 8 (over x, core).
Axes of the slice: x: 4, y: 4, z: 4, core: 2. Of those that a mesh axis runs over, the one named last changes fastest.
Arguments:
- blocks: bfloat16 [2048, 4096], P('req'), may hold values from -6 to 6
- token_embed: bfloat16 [2048, 4096], P('req'), may hold values from -6 to 6
- accepted: int32 [2048], P('req'), may hold values 0 or 1
- prompt_len: int32 [16], P('req'), may hold values from 2 to 512, as said below
- cache_len: int32 [16, 8], P('req'), may hold values from 1 to 1024, as said below
- prompt_kv: bfloat16 [16, 512, 2048], P('req', None, 'mlp'), may hold values from -364 to 364
- cache_kv: bfloat16 [16, 8, 1024, 2048], P('req', None, None, 'mlp'), may hold values from -6 to 6
- attn_gain: float32 [4096], replicated, may hold values from 0.25 to 1.75
- w_q: bfloat16 [4096, 4096], P(None, 'mlp'), may hold values from -0.09375 to 0.09375
- w_kv: bfloat16 [4096, 2048], P(None, 'mlp'), may hold values from -0.09375 to 0.09375
- w_o: bfloat16 [4096, 4096], P('mlp'), may hold values from -0.09375 to 0.09375
- mlp_gain: float32 [4096], replicated, may hold values from 0.25 to 1.75
- w_gate: bfloat16 [4096, 7168], P('req', 'mlp'), may hold values from -0.09375 to 0.09375
- w_up: bfloat16 [4096, 7168], P('req', 'mlp'), may hold values from -0.09375 to 0.09375
- w_down: bfloat16 [7168, 4096], P('mlp'), may hold values from -0.0625 to 0.0625
Outputs:
- denoised: bfloat16 [2048, 4096], P('req')
The draws below stay inside these ranges and needn't reach their ends.
Inputs may be any that keep to these rules, and one draw needn't show every extreme that they name: `prompt_len`: shared by the 8 requests of a group; some group has a prompt of exactly 512. `cache_len`: every group has a request with exactly 1024 cached tokens.
All inputs are finite; a program needn't handle non-finite values. No bound on the sum of `accepted` on one device may be relied on, other than what follows from the above.
Results may differ from the reference program's by a relative error of at most 0.022.
Values may be sent and summed in bfloat16 or wider, within the bound.
A program may use at most 128 MiB of HBM per device.

```python
import math
import jax
import jax.numpy as jnp
from jax import lax

D = 4096
HEADS = 32
KV_HEADS = 8
HEAD_DIM = 128
FF = 7168
REQS = 8
BLOCK = 16
CACHE = 1024
PMAX = 512
GROUPS = 16
TOKENS = 2048


def draw_prompt_len(key, part):
    first_key, second_key = jax.random.split(jax.random.fold_in(key, 11))
    base = jax.random.randint(first_key, (GROUPS,), 2, PMAX + 1)
    chosen = jax.random.randint(second_key, (), 0, GROUPS)
    return jnp.where(jnp.arange(GROUPS) == chosen, PMAX, base).astype(jnp.int32)


def draw_cache_len(key, part):
    first_key, second_key = jax.random.split(jax.random.fold_in(key, 23))
    base = jax.random.randint(first_key, (GROUPS, REQS), 1, CACHE + 1)
    chosen = jax.random.randint(second_key, (GROUPS,), 0, REQS)
    return jnp.where(jnp.arange(REQS)[None, :] == chosen[:, None], CACHE, base).astype(jnp.int32)


def draw_prompt_kv(key, part):
    base_key = jax.random.fold_in(jax.random.fold_in(key, 37), 0)
    full_shape = (GROUPS, PMAX, 2 * KV_HEADS * HEAD_DIM)
    base = jnp.clip(jax.random.normal(base_key, full_shape, jnp.float32), -6.0, 6.0)
    return base.astype(jnp.bfloat16)


def set_ends(drawn, own_key, smallest, top_value):
    longest = drawn.shape.index(max(drawn.shape))
    spots = []
    for shift in (0, 1):
        where = [jax.random.randint(jax.random.fold_in(own_key, axis), (), 0, length) for axis, length in enumerate(drawn.shape)]
        where[longest] = (where[longest] + shift) % drawn.shape[longest]
        spots.append(tuple(where))
    return drawn.at[spots[0]].set(smallest).at[spots[1]].set(top_value)


def shard_levels(own_key, shape, pieces, least, top_value):
    level = 1.0
    for position, parts in pieces:
        draws = jax.random.uniform(jax.random.fold_in(jax.random.fold_in(own_key, 6), position), (parts,), jnp.float32, least / len(pieces), top_value / len(pieces))
        level = level * jnp.repeat(jnp.exp(draws), shape[position] // parts).reshape((-1,) + (1,) * (len(shape) - 1 - position))
    return level


def normal_values(rng, shape, scale, most, pieces=(), kind=jnp.bfloat16):
    values = jax.random.normal(rng, shape, jnp.float32) * scale
    if len(pieces) > 0:
        values = shard_levels(rng, shape, pieces, -0.22, 0.18) * values
    return jnp.clip(values, min=-most, max=most).astype(kind)


def setup_inputs(seed: int = 0) -> dict:
    key_of = jax.random.split(jax.random.key(seed), 16)
    return {
        "blocks": normal_values(key_of[0], (TOKENS, D), 1.0, 6.0, ((0, 16),)),
        "token_embed": normal_values(key_of[1], (TOKENS, D), 1.0, 6.0, ((0, 16),)),
        "accepted": set_ends((jax.random.randint(key_of[2], (TOKENS,), 0, 2) < 1).astype(jnp.int32), jax.random.fold_in(key_of[2], 1), 0, 1),
        "prompt_len": draw_prompt_len(jax.random.fold_in(key_of[15], 71), 0),
        "cache_len": draw_cache_len(jax.random.fold_in(key_of[15], 71), 0),
        "prompt_kv": draw_prompt_kv(jax.random.fold_in(key_of[15], 71), 0),
        "cache_kv": normal_values(key_of[6], (GROUPS, REQS, CACHE, 2 * KV_HEADS * HEAD_DIM), 1.0, 6.0, ((0, 16), (3, 8))),
        "attn_gain": jnp.clip(1.0 + 0.15 * jax.random.normal(key_of[7], (D,), jnp.float32), 0.25, 1.75),
        "w_q": normal_values(key_of[8], (D, HEADS * HEAD_DIM), D ** -0.5, 0.09375, ((1, 8),)),
        "w_kv": normal_values(key_of[9], (D, 2 * KV_HEADS * HEAD_DIM), D ** -0.5, 0.09375, ((1, 8),)),
        "w_o": normal_values(key_of[10], (HEADS * HEAD_DIM, D), (HEADS * HEAD_DIM) ** -0.5, 0.09375, ((0, 8),)),
        "mlp_gain": jnp.clip(1.0 + 0.15 * jax.random.normal(key_of[11], (D,), jnp.float32), 0.25, 1.75),
        "w_gate": normal_values(key_of[12], (D, FF), D ** -0.5, 0.09375, ((0, 16), (1, 8))),
        "w_up": normal_values(key_of[13], (D, FF), D ** -0.5, 0.09375, ((0, 16), (1, 8))),
        "w_down": normal_values(key_of[14], (FF, D), FF ** -0.5, 0.0625, ((0, 8),)),
    }


EPSILON = 1e-05
THETA = 500000.0

def rms_scale(stream, gain):
    widened = stream.astype(jnp.float32)
    mean_square = lax.optimization_barrier(jnp.mean(widened * widened, axis=-1, keepdims=True))
    return (widened * lax.rsqrt(mean_square + EPSILON) * gain.astype(jnp.float32)).astype(jnp.bfloat16)

def rope(values, positions):
    head_size = values.shape[-1]
    half_size = head_size // 2
    frequency = THETA ** (-2.0 * jnp.arange(half_size, dtype=jnp.float32) / head_size)
    angles = positions.astype(jnp.float32)[:, None] * frequency[None, :]
    cosine = jnp.cos(angles)[:, None, :]
    sine = jnp.sin(angles)[:, None, :]
    first = values[..., :half_size]
    second = values[..., half_size:]
    return jnp.concatenate([first * cosine - second * sine, second * cosine + first * sine], axis=-1)

def attend_one(queries, block_keys, block_values, prompt_part, cached_part, prompt_size, cache_size):
    block_len, head_count, head_size = queries.shape
    kv_heads = block_keys.shape[1]
    group_size = head_count // kv_heads
    grouped = queries.reshape(block_len, kv_heads, group_size, head_size).astype(jnp.float32)
    scale = 1.0 / math.sqrt(head_size)

    def scores(keys):
        return jnp.einsum('tkgd,lkd->kgtl', grouped, keys.astype(jnp.float32)) * scale
    prompt_score = scores(prompt_part[:, :, 0])
    cache_score = scores(cached_part[:, :, 0])
    block_score = scores(block_keys)
    prompt_ok = jnp.arange(prompt_part.shape[0], dtype=jnp.int32) < prompt_size
    cache_ok = jnp.arange(cached_part.shape[0], dtype=jnp.int32) < cache_size
    prompt_score = jnp.where(prompt_ok, prompt_score, -1e+30)
    cache_score = jnp.where(cache_ok, cache_score, -1e+30)
    largest = jnp.maximum(jnp.maximum(lax.optimization_barrier(jnp.max(prompt_score, -1, keepdims=True)), lax.optimization_barrier(jnp.max(cache_score, -1, keepdims=True))), lax.optimization_barrier(jnp.max(block_score, -1, keepdims=True)))
    prompt_exp = jnp.exp(prompt_score - largest)
    cache_exp = jnp.exp(cache_score - largest)
    block_exp = jnp.exp(block_score - largest)
    total = lax.optimization_barrier(jnp.sum(prompt_exp, -1, keepdims=True)) + lax.optimization_barrier(jnp.sum(cache_exp, -1, keepdims=True)) + lax.optimization_barrier(jnp.sum(block_exp, -1, keepdims=True))
    prompt_w = (prompt_exp / total).astype(jnp.bfloat16).astype(jnp.float32)
    cache_w = (cache_exp / total).astype(jnp.bfloat16).astype(jnp.float32)
    block_w = (block_exp / total).astype(jnp.bfloat16).astype(jnp.float32)
    result = jnp.einsum('kgtl,lkd->tkgd', prompt_w, prompt_part[:, :, 1].astype(jnp.float32))
    result = result + jnp.einsum('kgtl,lkd->tkgd', cache_w, cached_part[:, :, 1].astype(jnp.float32))
    result = result + jnp.einsum('kgtl,lkd->tkgd', block_w, block_values.astype(jnp.float32))
    return result.reshape(block_len, head_count * head_size).astype(jnp.bfloat16)

def reference(blocks, token_embed, accepted, prompt_len, cache_len, prompt_kv, cache_kv, attn_gain, w_q, w_kv, w_o, mlp_gain, w_gate, w_up, w_down):
    positions = (prompt_len[:, None, None] + cache_len[:, :, None] + jnp.arange(BLOCK, dtype=jnp.int32)[None, None, :]).reshape(-1).astype(jnp.int32)
    group_index = jnp.repeat(jnp.arange(GROUPS, dtype=jnp.int32), REQS)
    prompts = prompt_kv.reshape(GROUPS, PMAX, KV_HEADS, 2, HEAD_DIM)
    cached = cache_kv.reshape(GROUPS * REQS, CACHE, KV_HEADS, 2, HEAD_DIM)
    cache_sizes = cache_len.reshape(-1)
    w_both = jnp.concatenate([w_gate, w_up], axis=1)

    def one_pass(stream):
        normed = rms_scale(stream, attn_gain)
        queries = rope(jnp.dot(normed, w_q, preferred_element_type=jnp.float32).reshape(TOKENS, HEADS, HEAD_DIM), positions).astype(jnp.bfloat16)
        key_value = jnp.dot(normed, w_kv, preferred_element_type=jnp.float32).reshape(TOKENS, KV_HEADS, 2, HEAD_DIM)
        keys = rope(key_value[:, :, 0], positions).astype(jnp.bfloat16)
        values = key_value[:, :, 1].astype(jnp.bfloat16)

        def attend_request(items):
            query_part, key_part, value_part, cache_part, group, cache_size = items
            prompt_part = lax.dynamic_index_in_dim(prompts, group, 0, keepdims=False)
            prompt_size = lax.dynamic_index_in_dim(prompt_len, group, 0, keepdims=False)
            return attend_one(query_part, key_part, value_part, prompt_part, cache_part, prompt_size, cache_size)
        attended = lax.map(attend_request, (queries.reshape(GROUPS * REQS, BLOCK, HEADS, HEAD_DIM), keys.reshape(GROUPS * REQS, BLOCK, KV_HEADS, HEAD_DIM), values.reshape(GROUPS * REQS, BLOCK, KV_HEADS, HEAD_DIM), cached, group_index, cache_sizes))
        attended = attended.reshape(TOKENS, HEADS * HEAD_DIM)
        mixed = jnp.dot(attended, w_o, preferred_element_type=jnp.float32)
        after_attn = (stream.astype(jnp.float32) + mixed).astype(jnp.bfloat16)
        normed2 = rms_scale(after_attn, mlp_gain)
        gate_up = jnp.dot(normed2, w_both, preferred_element_type=jnp.float32)
        hidden = (jax.nn.silu(gate_up[:, :FF]) * gate_up[:, FF:]).astype(jnp.bfloat16)
        down = jnp.dot(hidden, w_down, preferred_element_type=jnp.float32)
        return (after_attn.astype(jnp.float32) + down).astype(jnp.bfloat16)
    first = one_pass(blocks)
    second_input = jnp.where(accepted[:, None] == 1, token_embed, first)
    return one_pass(second_input)
```

```python
import functools
import math

import jax
import jax.numpy as jnp
from jax import lax
from jax.experimental import pallas as pl
from jax.experimental.pallas import tpu as pltpu
from jax.sharding import PartitionSpec as P

D = 4096
HEAD_DIM = 128
HEADS = 4
REQS = 8
BLOCK = 16
ROWS = REQS * BLOCK
CACHE = 1024
PMAX = 512
HIDDEN = 896
SHARD = 256
OWN = 16
EPSILON = 1e-05
THETA = 500000.0
MESH = pl.DeviceIdType.MESH
N_RS = 4
RS_W = D // N_RS
N_AG = 2
AG_W = D // N_AG
F32 = jnp.float32
BF16 = jnp.bfloat16


def kernel(
    lens, cos, sin, accepted, attn_gain, mlp_gain,
    blocks, token, prompt, cache, w_q, w_kv, w_o, w_gate, w_up, w_down,
    out,
    x_v, tok_v, prm_v, cache_v, wq_v, wkv_v, wo_v, gate_v, up_v, wd_v,
    nrm, qkv, q_s, k_s, v_s, att, g_acc, u_acc, hid,
    part, sib_out, sib_in, x_out, x_in, res,
    load_sem, g_send, g_recv, sib_ss, sib_rs, x_ss, x_rs, agx_s, agx_r, ags_s, ags_r,
):
    r = lax.axis_index("req")
    m = lax.axis_index("mlp")
    y, z = lax.div(r, 4), lax.rem(r, 4)
    x, c = lax.div(m, 2), lax.rem(m, 2)

    def add4(v, d):
        return lax.rem(v + (d % 4), 4)

    def chip(d):
        return (r, add4(x, d) * 2 + c)

    sibling = (r, x * 2 + 1 - c)

    def plane(dy, dz):
        return (add4(y, dy) * 4 + add4(z, dz), m)

    my_half = pl.multiple_of(64 * c, 64)
    other_half = pl.multiple_of(64 * (1 - c), 64)
    my_rows = pl.multiple_of(64 * c + OWN * x, OWN)

    own_shard = pl.ds(pl.multiple_of(r * SHARD, SHARD), SHARD)
    loads = {}
    for i, (name, src, dst) in enumerate(
        [
            ("gate", w_gate, gate_v.at[own_shard]),
            ("up", w_up, up_v.at[own_shard]),
            ("blocks", blocks, x_v),
            ("wq", w_q, wq_v),
            ("wkv", w_kv, wkv_v),
            ("prompt", prompt, prm_v),
            ("cache", cache, cache_v),
            ("wo", w_o, wo_v),
            ("wd", w_down, wd_v),
            ("tok", token.at[pl.ds(my_rows, OWN)], tok_v),
        ]
    ):
        copy = pltpu.make_async_copy(src, dst, load_sem.at[i])
        copy.start()
        loads[name] = copy

    barrier = pltpu.get_barrier_semaphore()
    partners = [chip(1), chip(2), chip(3), sibling, plane(0, 1), plane(0, 3), plane(1, 0), plane(3, 0)]
    for who in partners:
        pl.semaphore_signal(barrier, inc=1, device_id=who, device_id_type=MESH)
    pl.semaphore_wait(barrier, len(partners))

    full = (gate_v, up_v)
    sends = ([], [])

    def index(mat, a, b):
        dy, dz = (b, a) if mat == 0 else (a, b)
        return add4(y, dy) * 4 + add4(z, dz)

    def piece(mat, a, b, half):
        start = index(mat, a, b) * SHARD
        if half is None:
            return full[mat].at[pl.ds(pl.multiple_of(start, SHARD), SHARD)]
        return full[mat].at[pl.ds(pl.multiple_of(start + half * (SHARD // 2), SHARD // 2), SHARD // 2)]

    def g_copy(mat, a, b, half, axis, step, send_sem):
        da, db = (step, 0) if axis == 0 else (0, step)
        dy, dz = (db, da) if mat == 0 else (da, db)
        ref = piece(mat, a, b, half)
        return pltpu.make_async_remote_copy(
            src_ref=ref,
            dst_ref=ref,
            send_sem=send_sem,
            recv_sem=g_recv.at[mat, (a - da) % 4, (b - db) % 4, half or 0],
            device_id=plane(dy, dz),
            device_id_type=MESH,
        )

    def g_start(mat, a, b, half, axis, step):
        copy = g_copy(mat, a, b, half, axis, step, g_send.at[mat, len(sends[mat])])
        copy.start()
        sends[mat].append(copy)

    def g_wait(mat, a, b, half=None):
        ref = piece(mat, a, b, half)
        pltpu.make_async_remote_copy(
            src_ref=ref,
            dst_ref=ref,
            send_sem=g_send.at[mat, 0],
            recv_sem=g_recv.at[mat, a % 4, b % 4, half or 0],
            device_id=plane(0, 1),
            device_id_type=MESH,
        ).wait_recv()

    def gather_0():
        loads["gate"].wait()
        loads["up"].wait()
        for axis in (0, 1):
            for mat in (0, 1):
                g_start(mat, 0, 0, None, axis, 1)
                g_start(mat, 0, 0, None, axis, -1)

    def gather_1():
        for mat in (0, 1):
            g_wait(mat, -1, 0)
            g_start(mat, -1, 0, 0, 0, 1)
            g_wait(mat, 1, 0)
            g_start(mat, 1, 0, 1, 0, -1)
        for a in (-1, 1):
            for mat in (0, 1):
                g_start(mat, a, 0, None, 1, 1)
                g_start(mat, a, 0, None, 1, -1)

    def forward(a):
        for mat in (0, 1):
            g_wait(mat, a, -1)
            g_start(mat, a, -1, 0, 1, 1)
            g_wait(mat, a, 1)
            g_start(mat, a, 1, 1, 1, -1)

    def gather_3():
        for mat in (0, 1):
            g_wait(mat, 2, 0, 0)
            g_wait(mat, 2, 0, 1)
            g_start(mat, 2, 0, None, 1, 1)
            g_start(mat, 2, 0, None, 1, -1)

    def norm_local():
        def step(i, carry):
            rows = pl.ds(pl.multiple_of(i * OWN, OWN), OWN)
            wide = x_v[rows, :].astype(F32)
            scale = lax.rsqrt(jnp.mean(wide * wide, axis=-1, keepdims=True) + EPSILON)
            nrm[rows, :] = (wide * scale * attn_gain[...]).astype(BF16)
            return carry

        lax.fori_loop(0, ROWS // OWN, step, 0)

    def project(ready):
        for k in range(N_AG):
            ready(k)
            cols = slice(k * AG_W, (k + 1) * AG_W)
            lhs = nrm[:, cols]
            q_part = jnp.dot(lhs, wq_v[cols, :], preferred_element_type=F32)
            kv_part = jnp.dot(lhs, wkv_v[cols, :], preferred_element_type=F32)
            if k == 0:
                qkv[:, : HEADS * HEAD_DIM] = q_part
                qkv[:, HEADS * HEAD_DIM :] = kv_part
            else:
                qkv[:, : HEADS * HEAD_DIM] += q_part
                qkv[:, HEADS * HEAD_DIM :] += kv_part

    def attention():
        def rope(values):
            return (values * cos[...] + pltpu.roll(values, HEAD_DIM // 2, 1) * sin[...]).astype(BF16)

        for h in range(HEADS):
            q_s[:, BLOCK * h : BLOCK * (h + 1), :] = rope(
                qkv[:, HEAD_DIM * h : HEAD_DIM * (h + 1)]
            ).reshape(REQS, BLOCK, HEAD_DIM)
        base = HEADS * HEAD_DIM
        k_s[...] = rope(qkv[:, base : base + HEAD_DIM]).reshape(REQS, BLOCK, HEAD_DIM)
        v_s[...] = qkv[:, base + HEAD_DIM :].astype(BF16).reshape(REQS, BLOCK, HEAD_DIM)
        scale = 1.0 / math.sqrt(HEAD_DIM)
        contract = (((1,), (1,)), ((), ()))

        def step(j, carry):
            q = q_s[j]

            def scores(keys):
                return lax.dot_general(q, keys, contract, preferred_element_type=F32) * scale

            s_c = scores(cache_v[j, :, :HEAD_DIM])
            s_p = scores(prm_v[:, :HEAD_DIM])
            s_b = scores(k_s[j])
            at_c = lax.broadcasted_iota(jnp.int32, s_c.shape, 1)
            at_p = lax.broadcasted_iota(jnp.int32, s_p.shape, 1)
            s_c = jnp.where(at_c < lens[1 + j], s_c, -1e30)
            s_p = jnp.where(at_p < lens[0], s_p, -1e30)
            top = jnp.maximum(
                jnp.maximum(jnp.max(s_c, -1, keepdims=True), jnp.max(s_p, -1, keepdims=True)),
                jnp.max(s_b, -1, keepdims=True),
            )
            e_c = jnp.exp(s_c - top)
            e_p = jnp.exp(s_p - top)
            e_b = jnp.exp(s_b - top)
            total = (
                jnp.sum(e_c, -1, keepdims=True)
                + jnp.sum(e_p, -1, keepdims=True)
                + jnp.sum(e_b, -1, keepdims=True)
            )
            mixed = jnp.dot(e_c.astype(BF16), cache_v[j, :, HEAD_DIM:], preferred_element_type=F32)
            mixed += jnp.dot(e_p.astype(BF16), prm_v[:, HEAD_DIM:], preferred_element_type=F32)
            mixed += jnp.dot(e_b.astype(BF16), v_s[j], preferred_element_type=F32)
            mixed = (mixed / total).astype(BF16)
            for h in range(HEADS):
                att[j, :, HEAD_DIM * h : HEAD_DIM * (h + 1)] = mixed[BLOCK * h : BLOCK * (h + 1)]
            return carry

        lax.fori_loop(0, REQS, step, 0)

    pending = []

    def reduce_scatter(lhs, weight):
        def chips(n):
            sib_copies[n].wait_recv()
            total = part[n, pl.ds(my_half, 64), :] + sib_in[n].astype(F32)
            part[n, pl.ds(my_half, 64), :] = total
            x_out[n] = total.astype(BF16).reshape(4, OWN, RS_W)
            for d in (2, 1, 3):
                copy = pltpu.make_async_remote_copy(
                    src_ref=x_out.at[n, add4(x, d)],
                    dst_ref=x_in.at[n, d],
                    send_sem=x_ss.at[n, d],
                    recv_sem=x_rs.at[n, d],
                    device_id=chip(d),
                    device_id_type=MESH,
                )
                copy.start()
                x_copies.append(copy)

        sib_copies, x_copies = [], []
        for n in range(N_RS):
            part[n] = jnp.dot(lhs, weight[:, n * RS_W : (n + 1) * RS_W], preferred_element_type=F32)
            sib_out[n] = part[n, pl.ds(other_half, 64), :].astype(BF16)
            copy = pltpu.make_async_remote_copy(
                src_ref=sib_out.at[n],
                dst_ref=sib_in.at[n],
                send_sem=sib_ss.at[n],
                recv_sem=sib_rs.at[n],
                device_id=sibling,
                device_id_type=MESH,
            )
            copy.start()
            sib_copies.append(copy)
            if n > 0:
                chips(n - 1)
        chips(N_RS - 1)

        def own(n):
            total = part[n, pl.ds(my_rows, OWN), :]
            for i, d in enumerate((2, 1, 3)):
                x_copies[3 * n + i].wait_recv()
                total = total + x_in[n, d].astype(F32)
            return total

        def finish():
            for copy in sib_copies + x_copies:
                copy.wait_send()

        return own, finish

    def normalize(square_sum, gain):
        scale = lax.rsqrt(square_sum / D + EPSILON)
        for n in range(N_RS):
            cols = slice(n * RS_W, (n + 1) * RS_W)
            nrm[pl.ds(my_rows, OWN), cols] = (res[:, cols] * scale * gain[:, cols]).astype(BF16)

    def share_rows():
        ag = {}

        def copy_rows(k, row, send, recv, who):
            ref = nrm.at[pl.ds(pl.multiple_of(row, OWN), OWN), pl.ds(k * AG_W, AG_W)]
            return pltpu.make_async_remote_copy(
                src_ref=ref, dst_ref=ref, send_sem=send, recv_sem=recv, device_id=who, device_id_type=MESH
            )

        for k in range(N_AG):
            for d in (2, 1, 3):
                ag[k, d] = copy_rows(k, my_rows, agx_s.at[k, d], agx_r.at[k, d], chip(d))
                ag[k, d].start()
            ag[k, 4] = copy_rows(k, my_rows, ags_s.at[k, 0], ags_r.at[k, 0], sibling)
            ag[k, 4].start()

        def ready(k):
            for d in (1, 3, 2):
                row = 64 * c + OWN * add4(x, -d)
                copy_rows(k, row, agx_s.at[k, d], agx_r.at[k, d], sibling).wait_recv()
                ag[k, 4 + d] = copy_rows(k, row, ags_s.at[k, d], ags_r.at[k, d], sibling)
                ag[k, 4 + d].start()
            for d in (0, 1, 3, 2):
                row = 64 * (1 - c) + OWN * add4(x, -d)
                copy_rows(k, row, ags_s.at[k, d], ags_r.at[k, d], sibling).wait_recv()

        def finish():
            for copy in ag.values():
                copy.wait_send()

        return ready, finish

    def after_attention(own, gain):
        square_sum = jnp.zeros((OWN, 1), F32)
        for n in range(N_RS):
            cols = slice(n * RS_W, (n + 1) * RS_W)
            total = (res[:, cols] + own(n)).astype(BF16).astype(F32)
            res[:, cols] = total
            square_sum += jnp.sum(total * total, axis=-1, keepdims=True)
        normalize(square_sum, gain)

    def between_passes(own):
        take = accepted[:, :1] == 1
        square_sum = jnp.zeros((OWN, 1), F32)
        for n in range(N_RS):
            cols = slice(n * RS_W, (n + 1) * RS_W)
            first = (res[:, cols] + own(n)).astype(BF16).astype(F32)
            total = jnp.where(take, tok_v[:, cols].astype(F32), first)
            res[:, cols] = total
            square_sum += jnp.sum(total * total, axis=-1, keepdims=True)
        normalize(square_sum, attn_gain)

    def activate():
        gate = g_acc[...]
        hid[...] = (gate / (1.0 + jnp.exp(-gate)) * u_acc[...]).astype(BF16)

    def gate_up_item(mat, a, b, fresh=False):
        acc = (g_acc, u_acc)[mat]
        at = pl.ds(pl.multiple_of(index(mat, a, b) * SHARD, SHARD), SHARD)
        product = jnp.dot(nrm[:, at], full[mat][at, :], preferred_element_type=F32)
        if fresh:
            acc[...] = product
        else:
            acc[...] += product

    def attended():
        return att[...].reshape(ROWS, HEADS * HEAD_DIM)

    gather_0()
    loads["blocks"].wait()
    norm_local()
    res[...] = x_v[pl.ds(my_rows, OWN), :].astype(F32)
    loads["wq"].wait()
    loads["wkv"].wait()
    project(lambda k: None)
    gather_1()
    loads["prompt"].wait()
    loads["cache"].wait()
    attention()
    loads["wo"].wait()
    own, rs_done = reduce_scatter(attended(), wo_v)
    forward(0)
    after_attention(own, mlp_gain)
    rs_done()
    ready, ag_done = share_rows()
    gather_3()
    for k in range(N_AG):
        ready(k)
    ag_done()
    for a in (0, -1, 1, 2):
        for mat in (0, 1):
            gate_up_item(mat, a, 0, fresh=a == 0)
    for b in (-1, 1):
        for mat in (0, 1):
            gate_up_item(mat, 0, b)
    for a in (-1, 1, 2):
        forward(a)
        for b in (-1, 1):
            for mat in (0, 1):
                gate_up_item(mat, a, b)
    for a in (0, -1, 1, 2):
        for mat in (0, 1):
            g_wait(mat, a, 2, 0)
            g_wait(mat, a, 2, 1)
            gate_up_item(mat, a, 2)
    for copy in sends[0] + sends[1]:
        copy.wait_send()
    activate()
    loads["wd"].wait()
    loads["tok"].wait()
    own, rs_done = reduce_scatter(hid[...], wd_v)
    between_passes(own)
    rs_done()

    ready, ag_done = share_rows()
    project(ready)
    ag_done()
    attention()
    own, rs_done = reduce_scatter(attended(), wo_v)
    after_attention(own, mlp_gain)
    rs_done()
    ready, ag_done = share_rows()
    for k in range(N_AG):
        ready(k)
        for part_k in range(2):
            start = k * AG_W + part_k * (AG_W // 2)
            at = slice(start, start + AG_W // 2)
            for acc, weight in ((g_acc, gate_v), (u_acc, up_v)):
                product = jnp.dot(nrm[:, at], weight[at, :], preferred_element_type=F32)
                if start == 0:
                    acc[...] = product
                else:
                    acc[...] += product
    ag_done()
    activate()
    own, rs_done = reduce_scatter(hid[...], wd_v)
    for n in range(N_RS):
        cols = slice(n * RS_W, (n + 1) * RS_W)
        nrm[pl.ds(my_rows, OWN), cols] = (res[:, cols] + own(n)).astype(BF16)
    rs_done()
    ready, ag_done = share_rows()
    for k in range(N_AG):
        ready(k)
    ag_done()
    copy = pltpu.make_async_copy(nrm, out, load_sem.at[0])
    copy.start()
    copy.wait()


def body(
    blocks, token_embed, accepted, prompt_len, cache_len, prompt_kv, cache_kv, attn_gain,
    w_q, w_kv, w_o, mlp_gain, w_gate, w_up, w_down,
):
    prompt_size = prompt_len[0]
    cache_sizes = cache_len[0]
    positions = (
        prompt_size + cache_sizes[:, None] + jnp.arange(BLOCK, dtype=jnp.int32)[None, :]
    ).reshape(-1)
    half = HEAD_DIM // 2
    frequency = THETA ** (-2.0 * jnp.arange(half, dtype=F32) / HEAD_DIM)
    angles = positions.astype(F32)[:, None] * frequency[None, :]
    cosine, sine = jnp.cos(angles), jnp.sin(angles)
    cos = jnp.concatenate([cosine, cosine], axis=-1)
    sin = jnp.concatenate([-sine, sine], axis=-1)
    m = lax.axis_index("mlp")
    start = 64 * (m % 2) + OWN * (m // 2)
    taken = jnp.broadcast_to(lax.dynamic_slice(accepted, (start,), (OWN,))[:, None], (OWN, 128))
    lens = jnp.concatenate([prompt_len, cache_sizes])

    vmem = pl.BlockSpec(memory_space=pltpu.VMEM)
    anywhere = pl.BlockSpec(memory_space=pl.ANY)
    dma = pltpu.SemaphoreType.DMA
    return pl.pallas_call(
        kernel,
        out_shape=jax.ShapeDtypeStruct((ROWS, D), BF16),
        in_specs=[pl.BlockSpec(memory_space=pltpu.SMEM)] + [vmem] * 5 + [anywhere] * 10,
        out_specs=anywhere,
        scratch_shapes=[
            pltpu.VMEM((ROWS, D), BF16),
            pltpu.VMEM((OWN, D), BF16),
            pltpu.VMEM((PMAX, 2 * HEAD_DIM), BF16),
            pltpu.VMEM((REQS, CACHE, 2 * HEAD_DIM), BF16),
            pltpu.VMEM((D, HEADS * HEAD_DIM), BF16),
            pltpu.VMEM((D, 2 * HEAD_DIM), BF16),
            pltpu.VMEM((HEADS * HEAD_DIM, D), BF16),
            pltpu.VMEM((D, HIDDEN), BF16),
            pltpu.VMEM((D, HIDDEN), BF16),
            pltpu.VMEM((HIDDEN, D), BF16),
            pltpu.VMEM((ROWS, D), BF16),
            pltpu.VMEM((ROWS, (HEADS + 2) * HEAD_DIM), F32),
            pltpu.VMEM((REQS, HEADS * BLOCK, HEAD_DIM), BF16),
            pltpu.VMEM((REQS, BLOCK, HEAD_DIM), BF16),
            pltpu.VMEM((REQS, BLOCK, HEAD_DIM), BF16),
            pltpu.VMEM((REQS, BLOCK, HEADS * HEAD_DIM), BF16),
            pltpu.VMEM((ROWS, HIDDEN), F32),
            pltpu.VMEM((ROWS, HIDDEN), F32),
            pltpu.VMEM((ROWS, HIDDEN), BF16),
            pltpu.VMEM((N_RS, ROWS, RS_W), F32),
            pltpu.VMEM((N_RS, 64, RS_W), BF16),
            pltpu.VMEM((N_RS, 64, RS_W), BF16),
            pltpu.VMEM((N_RS, 4, OWN, RS_W), BF16),
            pltpu.VMEM((N_RS, 4, OWN, RS_W), BF16),
            pltpu.VMEM((OWN, D), F32),
            dma((10,)),
            dma((2, 20)),
            dma((2, 4, 4, 2)),
            dma((N_RS,)),
            dma((N_RS,)),
            dma((N_RS, 4)),
            dma((N_RS, 4)),
            dma((N_AG, 4)),
            dma((N_AG, 4)),
            dma((N_AG, 4)),
            dma((N_AG, 4)),
        ],
        compiler_params=pltpu.CompilerParams(
            collective_id=0, has_side_effects=True, vmem_limit_bytes=60 * 2**20
        ),
        name="two_passes",
    )(
        lens, cos, sin, taken, attn_gain[None, :], mlp_gain[None, :],
        blocks, token_embed, prompt_kv[0], cache_kv[0], w_q, w_kv, w_o, w_gate, w_up, w_down,
    )


def solution(mesh):
    return jax.shard_map(
        body,
        mesh=mesh,
        in_specs=(
            P("req", None),
            P("req", None),
            P("req"),
            P("req"),
            P("req", None),
            P("req", None, "mlp"),
            P("req", None, None, "mlp"),
            P(),
            P(None, "mlp"),
            P(None, "mlp"),
            P("mlp", None),
            P(),
            P("req", "mlp"),
            P("req", "mlp"),
            P("mlp", None),
        ),
        out_specs=P("req", None),
        check_vma=False,
    )
```

```python
import math

import jax
import jax.numpy as jnp
from jax import lax
from jax.experimental import pallas as pl
from jax.experimental.pallas import tpu as pltpu
from jax.sharding import PartitionSpec as P
import numpy as np

D = 4096
HEAD_DIM = 128
HEADS = 4
REQS = 8
BLOCK = 16
ROWS = REQS * BLOCK
CACHE = 1024
PMAX = 512
HIDDEN = 896
SHARD = 256
SLICE = 1024
OWN = 16
EPSILON = 1e-05
THETA = 500000.0
MESH = pl.DeviceIdType.MESH
N_RS = 4
RS_W = D // N_RS
N_AG = 2
AG_W = D // N_AG
F32 = jnp.float32
BF16 = jnp.bfloat16


def kernel(
    prompt_len, cache_len, accepted, frequency, attn_gain, mlp_gain,
    blocks, token, prompt, cache, w_q, w_kv, w_o, w_gate, w_up, w_down,
    out,
    x_v, tok_v, prm_v, cache_v, wq_v, wkv_v, wo_v, gate_v, up_v, wd_v,
    nrm, qkv, q_s, k_s, v_s, att, g_acc, u_acc, hid,
    part, sib_out, sib_in, x_out, x_in, res, cos, sin,
    rows_k, far_out, far_in, near_out, near_in,
    load_sem, g_send, g_recv, sib_ss, sib_rs, x_ss, x_rs, agx_s, agx_r, ags_s, ags_r,
    ky_s, ky_r, kx_s, kx_r, ks_s, ks_r, far_s, far_r, near_s, near_r,
):
    r = lax.axis_index("req")
    m = lax.axis_index("mlp")
    y, z = lax.div(r, 4), lax.rem(r, 4)
    x, c = lax.div(m, 2), lax.rem(m, 2)

    def add4(v, d):
        return lax.rem(v + (d % 4), 4)

    def chip(d):
        return (r, add4(x, d) * 2 + c)

    sibling = (r, x * 2 + 1 - c)

    def plane(dy, dz):
        return (add4(y, dy) * 4 + add4(z, dz), m)

    my_half = pl.multiple_of(64 * c, 64)
    other_half = pl.multiple_of(64 * (1 - c), 64)
    my_rows = pl.multiple_of(64 * c + OWN * x, OWN)

    own_shard = pl.ds(pl.multiple_of(r * SHARD, SHARD), SHARD)
    loads = {}
    for i, (name, src, dst) in enumerate(
        [
            ("gate", w_gate, gate_v.at[own_shard]),
            ("up", w_up, up_v.at[own_shard]),
            ("blocks", blocks, x_v),
            ("wq", w_q, wq_v),
            ("wkv", w_kv, wkv_v),
            ("prompt", prompt, prm_v),
            ("cache", cache, cache_v),
            ("wo", w_o, wo_v),
            ("wd", w_down, wd_v),
            ("tok", token.at[pl.ds(my_rows, OWN)], tok_v),
        ]
    ):
        copy = pltpu.make_async_copy(src, dst, load_sem.at[i])
        copy.start()
        loads[name] = copy

    barrier = pltpu.get_barrier_semaphore()
    partners = [chip(1), chip(2), chip(3), sibling, plane(0, 1), plane(0, 3), plane(1, 0), plane(3, 0), plane(2, 0)]
    for who in partners:
        pl.semaphore_signal(barrier, inc=1, device_id=who, device_id_type=MESH)
    pl.semaphore_wait(barrier, len(partners))

    full = (gate_v, up_v)
    sends = ([], [])

    def index(mat, a, b):
        dy, dz = (b, a) if mat == 0 else (a, b)
        return add4(y, dy) * 4 + add4(z, dz)

    def piece(mat, a, b, half):
        start = index(mat, a, b) * SHARD
        if half is None:
            return full[mat].at[pl.ds(pl.multiple_of(start, SHARD), SHARD)]
        return full[mat].at[pl.ds(pl.multiple_of(start + half * (SHARD // 2), SHARD // 2), SHARD // 2)]

    def g_copy(mat, a, b, half, axis, step, send_sem):
        da, db = (step, 0) if axis == 0 else (0, step)
        dy, dz = (db, da) if mat == 0 else (da, db)
        ref = piece(mat, a, b, half)
        return pltpu.make_async_remote_copy(
            src_ref=ref,
            dst_ref=ref,
            send_sem=send_sem,
            recv_sem=g_recv.at[mat, (a - da) % 4, (b - db) % 4, half or 0],
            device_id=plane(dy, dz),
            device_id_type=MESH,
        )

    def g_start(mat, a, b, half, axis, step):
        copy = g_copy(mat, a, b, half, axis, step, g_send.at[mat, len(sends[mat])])
        copy.start()
        sends[mat].append(copy)

    def g_wait(mat, a, b, half=None):
        ref = piece(mat, a, b, half)
        pltpu.make_async_remote_copy(
            src_ref=ref,
            dst_ref=ref,
            send_sem=g_send.at[mat, 0],
            recv_sem=g_recv.at[mat, a % 4, b % 4, half or 0],
            device_id=plane(0, 1),
            device_id_type=MESH,
        ).wait_recv()

    def gather_0():
        loads["gate"].wait()
        loads["up"].wait()
        for axis in (0, 1):
            for mat in (0, 1):
                g_start(mat, 0, 0, None, axis, 1)
                g_start(mat, 0, 0, None, axis, -1)

    def turn(mat, axis):
        for step, half in ((1, 0), (-1, 1)):
            at = (-step, 0) if axis == 0 else (0, -step)
            g_wait(mat, *at)
            g_start(mat, *at, half, axis, step)

    def spread(mat, a):
        g_start(mat, a, 0, None, 1, 1)
        g_start(mat, a, 0, None, 1, -1)

    def halves(mat, a, b):
        g_wait(mat, a, b, 0)
        g_wait(mat, a, b, 1)

    def forward(mat, a):
        g_wait(mat, a, -1)
        g_start(mat, a, -1, 0, 1, 1)
        g_wait(mat, a, 1)
        g_start(mat, a, 1, 1, 1, -1)

    def tables():
        lane = lax.broadcasted_iota(jnp.int32, (BLOCK, HEAD_DIM), 1)
        row = lax.broadcasted_iota(jnp.int32, (BLOCK, HEAD_DIM), 0)
        for j in range(REQS):
            position = row + (prompt_len[0] + cache_len[0, j])
            angle = position.astype(F32) * frequency[...]
            cos[BLOCK * j : BLOCK * (j + 1), :] = jnp.cos(angle)
            sine = jnp.sin(angle)
            sin[BLOCK * j : BLOCK * (j + 1), :] = jnp.where(lane < HEAD_DIM // 2, -sine, sine)

    def norm_local():
        def step(i, carry):
            rows = pl.ds(pl.multiple_of(i * OWN, OWN), OWN)
            wide = x_v[rows, :].astype(F32)
            scale = lax.rsqrt(jnp.mean(wide * wide, axis=-1, keepdims=True) + EPSILON)
            nrm[rows, :] = (wide * scale * attn_gain[...]).astype(BF16)
            return carry

        lax.fori_loop(0, ROWS // OWN, step, 0)

    def project(ready):
        for k in range(N_AG):
            ready(k)
            cols = slice(k * AG_W, (k + 1) * AG_W)
            lhs = nrm[:, cols]
            q_part = jnp.dot(lhs, wq_v[cols, :], preferred_element_type=F32)
            kv_part = jnp.dot(lhs, wkv_v[cols, :], preferred_element_type=F32)
            if k == 0:
                qkv[:, : HEADS * HEAD_DIM] = q_part
                qkv[:, HEADS * HEAD_DIM :] = kv_part
            else:
                qkv[:, : HEADS * HEAD_DIM] += q_part
                qkv[:, HEADS * HEAD_DIM :] += kv_part

    def attention():
        def rope(values):
            return (values * cos[...] + pltpu.roll(values, HEAD_DIM // 2, 1) * sin[...]).astype(BF16)

        for h in range(HEADS):
            q_s[:, BLOCK * h : BLOCK * (h + 1), :] = rope(
                qkv[:, HEAD_DIM * h : HEAD_DIM * (h + 1)]
            ).reshape(REQS, BLOCK, HEAD_DIM)
        base = HEADS * HEAD_DIM
        k_s[...] = rope(qkv[:, base : base + HEAD_DIM]).reshape(REQS, BLOCK, HEAD_DIM)
        v_s[...] = qkv[:, base + HEAD_DIM :].astype(BF16).reshape(REQS, BLOCK, HEAD_DIM)
        scale = 1.0 / math.sqrt(HEAD_DIM)
        contract = (((1,), (1,)), ((), ()))

        def step(j, carry):
            q = q_s[j]

            def scores(keys):
                return lax.dot_general(q, keys, contract, preferred_element_type=F32) * scale

            s_c = scores(cache_v[j, :, :HEAD_DIM])
            s_p = scores(prm_v[:, :HEAD_DIM])
            s_b = scores(k_s[j])
            at_c = lax.broadcasted_iota(jnp.int32, s_c.shape, 1)
            at_p = lax.broadcasted_iota(jnp.int32, s_p.shape, 1)
            s_c = jnp.where(at_c < cache_len[0, j], s_c, -1e30)
            s_p = jnp.where(at_p < prompt_len[0], s_p, -1e30)
            top = jnp.maximum(
                jnp.maximum(jnp.max(s_c, -1, keepdims=True), jnp.max(s_p, -1, keepdims=True)),
                jnp.max(s_b, -1, keepdims=True),
            )
            e_c = jnp.exp(s_c - top)
            e_p = jnp.exp(s_p - top)
            e_b = jnp.exp(s_b - top)
            total = (
                jnp.sum(e_c, -1, keepdims=True)
                + jnp.sum(e_p, -1, keepdims=True)
                + jnp.sum(e_b, -1, keepdims=True)
            )
            mixed = jnp.dot(e_c.astype(BF16), cache_v[j, :, HEAD_DIM:], preferred_element_type=F32)
            mixed += jnp.dot(e_p.astype(BF16), prm_v[:, HEAD_DIM:], preferred_element_type=F32)
            mixed += jnp.dot(e_b.astype(BF16), v_s[j], preferred_element_type=F32)
            mixed = (mixed / total).astype(BF16)
            for h in range(HEADS):
                att[j, :, HEAD_DIM * h : HEAD_DIM * (h + 1)] = mixed[BLOCK * h : BLOCK * (h + 1)]
            return carry

        lax.fori_loop(0, REQS, step, 0)

    pending = []

    def reduce_scatter(lhs, weight):
        def chips(n):
            sib_copies[n].wait_recv()
            total = part[n, pl.ds(my_half, 64), :] + sib_in[n].astype(F32)
            part[n, pl.ds(my_half, 64), :] = total
            x_out[n] = total.astype(BF16).reshape(4, OWN, RS_W)
            for d in (2, 1, 3):
                copy = pltpu.make_async_remote_copy(
                    src_ref=x_out.at[n, add4(x, d)],
                    dst_ref=x_in.at[n, d],
                    send_sem=x_ss.at[n, d],
                    recv_sem=x_rs.at[n, d],
                    device_id=chip(d),
                    device_id_type=MESH,
                )
                copy.start()
                x_copies.append(copy)

        sib_copies, x_copies = [], []
        for n in range(N_RS):
            part[n] = jnp.dot(lhs, weight[:, n * RS_W : (n + 1) * RS_W], preferred_element_type=F32)
            sib_out[n] = part[n, pl.ds(other_half, 64), :].astype(BF16)
            copy = pltpu.make_async_remote_copy(
                src_ref=sib_out.at[n],
                dst_ref=sib_in.at[n],
                send_sem=sib_ss.at[n],
                recv_sem=sib_rs.at[n],
                device_id=sibling,
                device_id_type=MESH,
            )
            copy.start()
            sib_copies.append(copy)
            if n > 0:
                chips(n - 1)
        chips(N_RS - 1)

        def own(n):
            total = part[n, pl.ds(my_rows, OWN), :]
            for i, d in enumerate((2, 1, 3)):
                x_copies[3 * n + i].wait_recv()
                total = total + x_in[n, d].astype(F32)
            return total

        def finish():
            for copy in sib_copies + x_copies:
                copy.wait_send()

        return own, finish

    def normalize(square_sum, gain):
        scale = lax.rsqrt(square_sum / D + EPSILON)
        for n in range(N_RS):
            cols = slice(n * RS_W, (n + 1) * RS_W)
            nrm[pl.ds(my_rows, OWN), cols] = (res[:, cols] * scale * gain[:, cols]).astype(BF16)

    def share_rows():
        ag = {}

        def copy_rows(k, row, send, recv, who):
            ref = nrm.at[pl.ds(pl.multiple_of(row, OWN), OWN), pl.ds(k * AG_W, AG_W)]
            return pltpu.make_async_remote_copy(
                src_ref=ref, dst_ref=ref, send_sem=send, recv_sem=recv, device_id=who, device_id_type=MESH
            )

        for k in range(N_AG):
            for d in (2, 1, 3):
                ag[k, d] = copy_rows(k, my_rows, agx_s.at[k, d], agx_r.at[k, d], chip(d))
                ag[k, d].start()
            ag[k, 4] = copy_rows(k, my_rows, ags_s.at[k, 0], ags_r.at[k, 0], sibling)
            ag[k, 4].start()

        def ready(k):
            for d in (1, 3, 2):
                row = 64 * c + OWN * add4(x, -d)
                copy_rows(k, row, agx_s.at[k, d], agx_r.at[k, d], sibling).wait_recv()
                ag[k, 4 + d] = copy_rows(k, row, ags_s.at[k, d], ags_r.at[k, d], sibling)
                ag[k, 4 + d].start()
            for d in (0, 1, 3, 2):
                row = 64 * (1 - c) + OWN * add4(x, -d)
                copy_rows(k, row, ags_s.at[k, d], ags_r.at[k, d], sibling).wait_recv()

        def finish():
            for copy in ag.values():
                copy.wait_send()

        return ready, finish

    def after_attention(own, gain):
        square_sum = jnp.zeros((OWN, 1), F32)
        for n in range(N_RS):
            cols = slice(n * RS_W, (n + 1) * RS_W)
            total = (res[:, cols] + own(n)).astype(BF16).astype(F32)
            res[:, cols] = total
            square_sum += jnp.sum(total * total, axis=-1, keepdims=True)
        normalize(square_sum, gain)

    def between_passes(own):
        lane = lax.broadcasted_iota(jnp.int32, (OWN, ROWS), 1)
        row = lax.broadcasted_iota(jnp.int32, (OWN, ROWS), 0) + my_rows
        mine = jnp.where(lane == row, accepted[...].astype(F32), 0.0)
        take = jnp.sum(mine, axis=-1, keepdims=True) == 1.0
        square_sum = jnp.zeros((OWN, 1), F32)
        for n in range(N_RS):
            cols = slice(n * RS_W, (n + 1) * RS_W)
            first = (res[:, cols] + own(n)).astype(BF16).astype(F32)
            total = jnp.where(take, tok_v[:, cols].astype(F32), first)
            res[:, cols] = total
            square_sum += jnp.sum(total * total, axis=-1, keepdims=True)
        normalize(square_sum, attn_gain)

    def activate():
        gate = g_acc[...]
        hid[...] = (gate / (1.0 + jnp.exp(-gate)) * u_acc[...]).astype(BF16)

    def slice_rows():
        made = {}

        def go(key, src, dst, send, recv, who):
            made[key] = pltpu.make_async_remote_copy(
                src_ref=src, dst_ref=dst, send_sem=send, recv_sem=recv, device_id=who, device_id_type=MESH
            )
            made[key].start()

        def rows_of(k, core, d):
            row = 64 * core + OWN * add4(x, d)
            return rows_k.at[k, pl.ds(pl.multiple_of(row, OWN), OWN)]

        def chunk(dy):
            return pl.ds(pl.multiple_of(add4(y, dy) * SLICE, SLICE), SLICE)

        def over_x(k):
            for d in (2, 1, 3):
                go(("x", k, d), rows_of(k, c, 0), rows_of(k, c, 0), kx_s.at[k, d], kx_r.at[k, d], chip(d))
            go(("s", k, 0), rows_of(k, c, 0), rows_of(k, c, 0), ks_s.at[k, 0], ks_r.at[k, 0], sibling)

        for dy in (2, 1, 3):
            k = (-dy) % 4
            src = nrm.at[pl.ds(my_rows, OWN), chunk(dy)]
            go(("y", k), src, rows_of(k, c, 0), ky_s.at[k], ky_r.at[k], plane(dy, 0))
        rows_k[0, pl.ds(my_rows, OWN), :] = nrm[pl.ds(my_rows, OWN), chunk(0)]
        over_x(0)
        for k in (2, 1, 3):
            made["y", k].wait_recv()
            over_x(k)

        def ready(k):
            for d in (1, 3, 2):
                made["x", k, d].wait_recv()
                ref = rows_of(k, c, -d)
                go(("s", k, d), ref, ref, ks_s.at[k, d], ks_r.at[k, d], sibling)
            for d in (0, 1, 3, 2):
                made["s", k, d].wait_recv()

        def finish():
            for copy in made.values():
                copy.wait_send()

        return ready, finish

    def slice_gate_up(ready):
        made = []
        at = pl.ds(pl.multiple_of(y * SLICE, SLICE), SLICE)

        def product(k, mat):
            return jnp.dot(rows_k[k], full[mat][at, :], preferred_element_type=F32)

        def go(src, dst, send, recv, dy):
            copy = pltpu.make_async_remote_copy(
                src_ref=src, dst_ref=dst, send_sem=send, recv_sem=recv,
                device_id=plane(dy, 0), device_id_type=MESH,
            )
            copy.start()
            made.append(copy)
            return copy

        ready(2)
        far = []
        for mat in (0, 1):
            far_out[mat] = product(2, mat).astype(BF16)
            far.append(
                go(far_out.at[mat], far_in.at[mat], far_s.at[mat], far_r.at[mat], 1 - 2 * mat)
            )
        near = []

        def send_near(i, mat, value):
            near_out[i, mat] = value.astype(BF16)
            near.append(
                go(
                    near_out.at[i, mat], near_in.at[i, mat],
                    near_s.at[i, mat], near_r.at[i, mat], 1 - 2 * i,
                )
            )

        ready(1)
        send_near(0, 1, product(1, 1))
        ready(3)
        send_near(1, 0, product(3, 0))
        value = product(1, 0)
        far[0].wait_recv()
        send_near(0, 0, value + far_in[0].astype(F32))
        value = product(3, 1)
        far[1].wait_recv()
        send_near(1, 1, value + far_in[1].astype(F32))
        ready(0)
        for mat, acc in ((0, g_acc), (1, u_acc)):
            acc[...] = product(0, mat)

        def collect():
            for copy in near:
                copy.wait_recv()
            for mat, acc in ((0, g_acc), (1, u_acc)):
                acc[...] += near_in[0, mat].astype(F32) + near_in[1, mat].astype(F32)

        def finish():
            for copy in made:
                copy.wait_send()

        return collect, finish

    def attended():
        return att[...].reshape(ROWS, HEADS * HEAD_DIM)

    gather_0()
    tables()
    loads["blocks"].wait()
    norm_local()
    res[...] = x_v[pl.ds(my_rows, OWN), :].astype(F32)
    loads["wq"].wait()
    loads["wkv"].wait()
    project(lambda k: None)
    loads["prompt"].wait()
    loads["cache"].wait()
    attention()
    loads["wo"].wait()
    own, rs_done = reduce_scatter(attended(), wo_v)
    turn(0, 0)
    turn(1, 1)
    turn(1, 0)
    turn(0, 1)
    after_attention(own, mlp_gain)
    rs_done()
    ready, rows_done = slice_rows()
    halves(0, 2, 0)
    halves(1, 0, 2)
    collect, sums_done = slice_gate_up(ready)
    halves(1, 2, 0)
    for a in (-1, 1, 2):
        spread(1, a)
    collect()
    for a in (-1, 1, 2):
        spread(0, a)
    rows_done()
    sums_done()
    activate()
    loads["wd"].wait()
    loads["tok"].wait()
    own, rs_done = reduce_scatter(hid[...], wd_v)
    between_passes(own)
    rs_done()

    ready, ag_done = share_rows()
    project(ready)
    ag_done()
    for a in (-1, 1, 2):
        forward(1, a)
    attention()
    own, rs_done = reduce_scatter(attended(), wo_v)
    for a in (-1, 1):
        forward(0, a)
    after_attention(own, mlp_gain)
    rs_done()
    ready, ag_done = share_rows()
    forward(0, 2)
    halves(0, 0, 2)
    for a in (-1, 1, 2):
        halves(0, a, 2)
        halves(1, a, 2)
    for k in range(N_AG):
        ready(k)
        for part_k in range(2):
            start = k * AG_W + part_k * (AG_W // 2)
            at = slice(start, start + AG_W // 2)
            for acc, weight in ((g_acc, gate_v), (u_acc, up_v)):
                product = jnp.dot(nrm[:, at], weight[at, :], preferred_element_type=F32)
                if start == 0:
                    acc[...] = product
                else:
                    acc[...] += product
    ag_done()
    for copy in sends[0] + sends[1]:
        copy.wait_send()
    activate()
    own, rs_done = reduce_scatter(hid[...], wd_v)
    for n in range(N_RS):
        cols = slice(n * RS_W, (n + 1) * RS_W)
        nrm[pl.ds(my_rows, OWN), cols] = (res[:, cols] + own(n)).astype(BF16)
    rs_done()
    ready, ag_done = share_rows()
    for k in range(N_AG):
        ready(k)
    ag_done()
    copy = pltpu.make_async_copy(nrm, out, load_sem.at[0])
    copy.start()
    copy.wait()


def body(
    blocks, token_embed, accepted, prompt_len, cache_len, prompt_kv, cache_kv, attn_gain,
    w_q, w_kv, w_o, mlp_gain, w_gate, w_up, w_down,
):
    half = np.arange(HEAD_DIM // 2, dtype=np.float32)
    frequency = np.float32(THETA) ** (np.float32(-2.0) * half / np.float32(HEAD_DIM))
    frequency = jnp.asarray(np.concatenate([frequency, frequency])[None, :], dtype=F32)

    vmem = pl.BlockSpec(memory_space=pltpu.VMEM)
    anywhere = pl.BlockSpec(memory_space=pl.ANY)
    dma = pltpu.SemaphoreType.DMA
    return pl.pallas_call(
        kernel,
        out_shape=jax.ShapeDtypeStruct((ROWS, D), BF16),
        in_specs=[pl.BlockSpec(memory_space=pltpu.SMEM)] * 2 + [vmem] * 4 + [anywhere] * 10,
        out_specs=anywhere,
        scratch_shapes=[
            pltpu.VMEM((ROWS, D), BF16),
            pltpu.VMEM((OWN, D), BF16),
            pltpu.VMEM((PMAX, 2 * HEAD_DIM), BF16),
            pltpu.VMEM((REQS, CACHE, 2 * HEAD_DIM), BF16),
            pltpu.VMEM((D, HEADS * HEAD_DIM), BF16),
            pltpu.VMEM((D, 2 * HEAD_DIM), BF16),
            pltpu.VMEM((HEADS * HEAD_DIM, D), BF16),
            pltpu.VMEM((D, HIDDEN), BF16),
            pltpu.VMEM((D, HIDDEN), BF16),
            pltpu.VMEM((HIDDEN, D), BF16),
            pltpu.VMEM((ROWS, D), BF16),
            pltpu.VMEM((ROWS, (HEADS + 2) * HEAD_DIM), F32),
            pltpu.VMEM((REQS, HEADS * BLOCK, HEAD_DIM), BF16),
            pltpu.VMEM((REQS, BLOCK, HEAD_DIM), BF16),
            pltpu.VMEM((REQS, BLOCK, HEAD_DIM), BF16),
            pltpu.VMEM((REQS, BLOCK, HEADS * HEAD_DIM), BF16),
            pltpu.VMEM((ROWS, HIDDEN), F32),
            pltpu.VMEM((ROWS, HIDDEN), F32),
            pltpu.VMEM((ROWS, HIDDEN), BF16),
            pltpu.VMEM((N_RS, ROWS, RS_W), F32),
            pltpu.VMEM((N_RS, 64, RS_W), BF16),
            pltpu.VMEM((N_RS, 64, RS_W), BF16),
            pltpu.VMEM((N_RS, 4, OWN, RS_W), BF16),
            pltpu.VMEM((N_RS, 4, OWN, RS_W), BF16),
            pltpu.VMEM((OWN, D), F32),
            pltpu.VMEM((ROWS, HEAD_DIM), F32),
            pltpu.VMEM((ROWS, HEAD_DIM), F32),
            pltpu.VMEM((4, ROWS, SLICE), BF16),
            pltpu.VMEM((2, ROWS, HIDDEN), BF16),
            pltpu.VMEM((2, ROWS, HIDDEN), BF16),
            pltpu.VMEM((2, 2, ROWS, HIDDEN), BF16),
            pltpu.VMEM((2, 2, ROWS, HIDDEN), BF16),
            dma((10,)),
            dma((2, 20)),
            dma((2, 4, 4, 2)),
            dma((N_RS,)),
            dma((N_RS,)),
            dma((N_RS, 4)),
            dma((N_RS, 4)),
            dma((N_AG, 4)),
            dma((N_AG, 4)),
            dma((N_AG, 4)),
            dma((N_AG, 4)),
            dma((4,)),
            dma((4,)),
            dma((4, 4)),
            dma((4, 4)),
            dma((4, 4)),
            dma((4, 4)),
            dma((2,)),
            dma((2,)),
            dma((2, 2)),
            dma((2, 2)),
        ],
        compiler_params=pltpu.CompilerParams(
            collective_id=0, has_side_effects=True, vmem_limit_bytes=60 * 2**20
        ),
        name="two_passes",
    )(
        prompt_len, cache_len, accepted[None, :], frequency, attn_gain[None, :], mlp_gain[None, :],
        blocks, token_embed, prompt_kv[0], cache_kv[0], w_q, w_kv, w_o, w_gate, w_up, w_down,
    )


def solution(mesh):
    return jax.shard_map(
        body,
        mesh=mesh,
        in_specs=(
            P("req", None),
            P("req", None),
            P("req"),
            P("req"),
            P("req", None),
            P("req", None, "mlp"),
            P("req", None, None, "mlp"),
            P(),
            P(None, "mlp"),
            P(None, "mlp"),
            P("mlp", None),
            P(),
            P("req", "mlp"),
            P("req", "mlp"),
            P("mlp", None),
        ),
        out_specs=P("req", None),
        check_vma=False,
    )
```

```python
import math

import jax
import jax.numpy as jnp
from jax import lax
from jax.experimental import pallas as pl
from jax.experimental.pallas import tpu as pltpu
from jax.sharding import PartitionSpec as P
import numpy as np

D = 4096
HEAD_DIM = 128
HEADS = 4
REQS = 8
BLOCK = 16
ROWS = REQS * BLOCK
CACHE = 1024
PMAX = 512
HIDDEN = 896
SHARD = 256
SLICE = 1024
OWN = 16
EPSILON = 1e-05
THETA = 500000.0
MESH = pl.DeviceIdType.MESH
N_RS = 4
RS_W = D // N_RS
N_AG = 2
AG_W = D // N_AG
F32 = jnp.float32
BF16 = jnp.bfloat16


def kernel(
    prompt_len, cache_len, accepted, frequency, attn_gain, mlp_gain,
    blocks, token, prompt, cache, w_q, w_kv, w_o, w_gate, w_up, w_down,
    out,
    x_v, tok_v, prm_v, cache_v, wq_v, wkv_v, wo_v, gate_v, up_v, wd_v,
    nrm, qkv, q_s, k_s, v_s, att, g_acc, u_acc, hid,
    part, sib_out, sib_in, x_out, x_in, res, cos, sin,
    rows_k, far_out, far_in, near_out, near_in,
    load_sem, g_send, g_recv, sib_ss, sib_rs, x_ss, x_rs, agx_s, agx_r, ags_s, ags_r,
    ky_s, ky_r, kx_s, kx_r, ks_s, ks_r, far_s, far_r, near_s, near_r,
):
    r = lax.axis_index("req")
    m = lax.axis_index("mlp")
    y, z = lax.div(r, 4), lax.rem(r, 4)
    x, c = lax.div(m, 2), lax.rem(m, 2)

    def add4(v, d):
        return lax.rem(v + (d % 4), 4)

    def chip(d):
        return (r, add4(x, d) * 2 + c)

    sibling = (r, x * 2 + 1 - c)

    def plane(dy, dz):
        return (add4(y, dy) * 4 + add4(z, dz), m)

    my_half = pl.multiple_of(64 * c, 64)
    other_half = pl.multiple_of(64 * (1 - c), 64)
    my_rows = pl.multiple_of(64 * c + OWN * x, OWN)

    own_shard = pl.ds(pl.multiple_of(r * SHARD, SHARD), SHARD)
    loads = {}
    for i, (name, src, dst) in enumerate(
        [
            ("gate", w_gate, gate_v.at[own_shard]),
            ("up", w_up, up_v.at[own_shard]),
            ("blocks", blocks, x_v),
            ("wq", w_q, wq_v),
            ("wkv", w_kv, wkv_v),
            ("prompt", prompt, prm_v),
            ("cache", cache, cache_v),
            ("wo", w_o, wo_v),
            ("wd", w_down, wd_v),
            ("tok", token.at[pl.ds(my_rows, OWN)], tok_v),
        ]
    ):
        copy = pltpu.make_async_copy(src, dst, load_sem.at[i])
        copy.start()
        loads[name] = copy

    barrier = pltpu.get_barrier_semaphore()
    partners = [chip(1), chip(2), chip(3), sibling, plane(0, 1), plane(0, 3), plane(1, 0), plane(3, 0), plane(2, 0)]
    for who in partners:
        pl.semaphore_signal(barrier, inc=1, device_id=who, device_id_type=MESH)
    pl.semaphore_wait(barrier, len(partners))

    full = (gate_v, up_v)
    sends = ([], [])

    def index(mat, a, b):
        dy, dz = (b, a) if mat == 0 else (a, b)
        return add4(y, dy) * 4 + add4(z, dz)

    def piece(mat, a, b, half):
        start = index(mat, a, b) * SHARD
        if half is None:
            return full[mat].at[pl.ds(pl.multiple_of(start, SHARD), SHARD)]
        return full[mat].at[pl.ds(pl.multiple_of(start + half * (SHARD // 2), SHARD // 2), SHARD // 2)]

    def g_copy(mat, a, b, half, axis, step, send_sem):
        da, db = (step, 0) if axis == 0 else (0, step)
        dy, dz = (db, da) if mat == 0 else (da, db)
        ref = piece(mat, a, b, half)
        return pltpu.make_async_remote_copy(
            src_ref=ref,
            dst_ref=ref,
            send_sem=send_sem,
            recv_sem=g_recv.at[mat, (a - da) % 4, (b - db) % 4, half or 0],
            device_id=plane(dy, dz),
            device_id_type=MESH,
        )

    def g_start(mat, a, b, half, axis, step):
        copy = g_copy(mat, a, b, half, axis, step, g_send.at[mat, len(sends[mat])])
        copy.start()
        sends[mat].append(copy)

    def g_wait(mat, a, b, half=None):
        ref = piece(mat, a, b, half)
        pltpu.make_async_remote_copy(
            src_ref=ref,
            dst_ref=ref,
            send_sem=g_send.at[mat, 0],
            recv_sem=g_recv.at[mat, a % 4, b % 4, half or 0],
            device_id=plane(0, 1),
            device_id_type=MESH,
        ).wait_recv()

    def gather_0():
        loads["gate"].wait()
        loads["up"].wait()
        for axis in (0, 1):
            for mat in (0, 1):
                g_start(mat, 0, 0, None, axis, 1)
                g_start(mat, 0, 0, None, axis, -1)

    def turn(mat, axis):
        for step, half in ((1, 0), (-1, 1)):
            at = (-step, 0) if axis == 0 else (0, -step)
            g_wait(mat, *at)
            g_start(mat, *at, half, axis, step)

    def spread(mat, a):
        g_start(mat, a, 0, None, 1, 1)
        g_start(mat, a, 0, None, 1, -1)

    def halves(mat, a, b):
        g_wait(mat, a, b, 0)
        g_wait(mat, a, b, 1)

    def forward(mat, a):
        g_wait(mat, a, -1)
        g_start(mat, a, -1, 0, 1, 1)
        g_wait(mat, a, 1)
        g_start(mat, a, 1, 1, 1, -1)

    def tables():
        lane = lax.broadcasted_iota(jnp.int32, (BLOCK, HEAD_DIM), 1)
        row = lax.broadcasted_iota(jnp.int32, (BLOCK, HEAD_DIM), 0)
        for j in range(REQS):
            position = row + (prompt_len[0] + cache_len[0, j])
            angle = position.astype(F32) * frequency[...]
            cos[BLOCK * j : BLOCK * (j + 1), :] = jnp.cos(angle)
            sine = jnp.sin(angle)
            sin[BLOCK * j : BLOCK * (j + 1), :] = jnp.where(lane < HEAD_DIM // 2, -sine, sine)

    def norm_local():
        def step(i, carry):
            rows = pl.ds(pl.multiple_of(i * OWN, OWN), OWN)
            wide = x_v[rows, :].astype(F32)
            scale = lax.rsqrt(jnp.mean(wide * wide, axis=-1, keepdims=True) + EPSILON)
            nrm[rows, :] = (wide * scale * attn_gain[...]).astype(BF16)
            return carry

        lax.fori_loop(0, ROWS // OWN, step, 0)

    def project(lo, hi):
        lhs = nrm[lo:hi, :]
        qkv[lo:hi, : HEADS * HEAD_DIM] = jnp.dot(lhs, wq_v[...], preferred_element_type=F32)
        qkv[lo:hi, HEADS * HEAD_DIM :] = jnp.dot(lhs, wkv_v[...], preferred_element_type=F32)

    def attention(lo, hi):
        first, last = lo // BLOCK, hi // BLOCK
        count = last - first

        def rope(values):
            turned = values * cos[lo:hi, :] + pltpu.roll(values, HEAD_DIM // 2, 1) * sin[lo:hi, :]
            return turned.astype(BF16).reshape(count, BLOCK, HEAD_DIM)

        for h in range(HEADS):
            q_s[first:last, BLOCK * h : BLOCK * (h + 1), :] = rope(
                qkv[lo:hi, HEAD_DIM * h : HEAD_DIM * (h + 1)]
            )
        base = HEADS * HEAD_DIM
        k_s[first:last] = rope(qkv[lo:hi, base : base + HEAD_DIM])
        v_s[first:last] = qkv[lo:hi, base + HEAD_DIM :].astype(BF16).reshape(count, BLOCK, HEAD_DIM)
        scale = math.log2(math.e) / math.sqrt(HEAD_DIM)
        contract = (((1,), (1,)), ((), ()))

        def step(j, carry):
            q = q_s[j]

            def scores(keys):
                return lax.dot_general(q, keys, contract, preferred_element_type=F32) * scale

            s_c = scores(cache_v[j, :, :HEAD_DIM])
            s_p = scores(prm_v[:, :HEAD_DIM])
            s_b = scores(k_s[j])
            at_c = lax.broadcasted_iota(jnp.int32, s_c.shape, 1)
            at_p = lax.broadcasted_iota(jnp.int32, s_p.shape, 1)
            s_c = jnp.where(at_c < cache_len[0, j], s_c, -1e30)
            s_p = jnp.where(at_p < prompt_len[0], s_p, -1e30)
            top = jnp.maximum(
                jnp.maximum(jnp.max(s_c, -1, keepdims=True), jnp.max(s_p, -1, keepdims=True)),
                jnp.max(s_b, -1, keepdims=True),
            )
            e_c = jnp.exp2(s_c - top)
            e_p = jnp.exp2(s_p - top)
            e_b = jnp.exp2(s_b - top)
            total = (
                jnp.sum(e_c, -1, keepdims=True)
                + jnp.sum(e_p, -1, keepdims=True)
                + jnp.sum(e_b, -1, keepdims=True)
            )
            mixed = jnp.dot(e_c.astype(BF16), cache_v[j, :, HEAD_DIM:], preferred_element_type=F32)
            mixed += jnp.dot(e_p.astype(BF16), prm_v[:, HEAD_DIM:], preferred_element_type=F32)
            mixed += jnp.dot(e_b.astype(BF16), v_s[j], preferred_element_type=F32)
            mixed = (mixed / total).astype(BF16)
            for h in range(HEADS):
                att[j, :, HEAD_DIM * h : HEAD_DIM * (h + 1)] = mixed[BLOCK * h : BLOCK * (h + 1)]
            return carry

        lax.fori_loop(first, last, step, 0, unroll=2)

    pending = []

    def reduce_scatter(lhs, weight):
        def chips(n):
            sib_copies[n].wait_recv()
            total = part[n, pl.ds(my_half, 64), :] + sib_in[n].astype(F32)
            part[n, pl.ds(my_half, 64), :] = total
            x_out[n] = total.astype(BF16).reshape(4, OWN, RS_W)
            for d in (2, 1, 3):
                copy = pltpu.make_async_remote_copy(
                    src_ref=x_out.at[n, add4(x, d)],
                    dst_ref=x_in.at[n, d],
                    send_sem=x_ss.at[n, d],
                    recv_sem=x_rs.at[n, d],
                    device_id=chip(d),
                    device_id_type=MESH,
                )
                copy.start()
                x_copies.append(copy)

        sib_copies, x_copies = [], []
        for n in range(N_RS):
            part[n] = jnp.dot(lhs, weight[:, n * RS_W : (n + 1) * RS_W], preferred_element_type=F32)
            sib_out[n] = part[n, pl.ds(other_half, 64), :].astype(BF16)
            copy = pltpu.make_async_remote_copy(
                src_ref=sib_out.at[n],
                dst_ref=sib_in.at[n],
                send_sem=sib_ss.at[n],
                recv_sem=sib_rs.at[n],
                device_id=sibling,
                device_id_type=MESH,
            )
            copy.start()
            sib_copies.append(copy)
            if n > 0:
                chips(n - 1)
        chips(N_RS - 1)

        def own(n):
            total = part[n, pl.ds(my_rows, OWN), :]
            for i, d in enumerate((2, 1, 3)):
                x_copies[3 * n + i].wait_recv()
                total = total + x_in[n, d].astype(F32)
            return total

        def finish():
            for copy in sib_copies + x_copies:
                copy.wait_send()

        return own, finish

    def normalize(square_sum, gain):
        scale = lax.rsqrt(square_sum / D + EPSILON)
        for n in range(N_RS):
            cols = slice(n * RS_W, (n + 1) * RS_W)
            nrm[pl.ds(my_rows, OWN), cols] = (res[:, cols] * scale * gain[:, cols]).astype(BF16)

    def after_attention(own, gain):
        square_sum = jnp.zeros((OWN, 1), F32)
        for n in range(N_RS):
            cols = slice(n * RS_W, (n + 1) * RS_W)
            total = (res[:, cols] + own(n)).astype(BF16).astype(F32)
            res[:, cols] = total
            square_sum += jnp.sum(total * total, axis=-1, keepdims=True)
        normalize(square_sum, gain)

    def between_passes(own):
        lane = lax.broadcasted_iota(jnp.int32, (OWN, ROWS), 1)
        row = lax.broadcasted_iota(jnp.int32, (OWN, ROWS), 0) + my_rows
        mine = jnp.where(lane == row, accepted[...].astype(F32), 0.0)
        take = jnp.sum(mine, axis=-1, keepdims=True) == 1.0
        square_sum = jnp.zeros((OWN, 1), F32)
        for n in range(N_RS):
            cols = slice(n * RS_W, (n + 1) * RS_W)
            first = (res[:, cols] + own(n)).astype(BF16).astype(F32)
            total = jnp.where(take, tok_v[:, cols].astype(F32), first)
            res[:, cols] = total
            square_sum += jnp.sum(total * total, axis=-1, keepdims=True)
        normalize(square_sum, attn_gain)

    def activate(lo, hi):
        gate = g_acc[lo:hi, :]
        hid[lo:hi, :] = (gate / (1.0 + jnp.exp(-gate)) * u_acc[lo:hi, :]).astype(BF16)

    def gate_up(lo, hi):
        lhs = nrm[lo:hi, :]
        g_acc[lo:hi, :] = jnp.dot(lhs, gate_v[...], preferred_element_type=F32)
        u_acc[lo:hi, :] = jnp.dot(lhs, up_v[...], preferred_element_type=F32)
        activate(lo, hi)

    def slice_rows():
        made = {}

        def go(key, src, dst, send, recv, who):
            made[key] = pltpu.make_async_remote_copy(
                src_ref=src, dst_ref=dst, send_sem=send, recv_sem=recv, device_id=who, device_id_type=MESH
            )
            made[key].start()

        def rows_of(k, core, d):
            row = 64 * core + OWN * add4(x, d)
            return rows_k.at[k, pl.ds(pl.multiple_of(row, OWN), OWN)]

        def chunk(dy):
            return pl.ds(pl.multiple_of(add4(y, dy) * SLICE, SLICE), SLICE)

        def over_x(k):
            for d in (2, 1, 3):
                go(("x", k, d), rows_of(k, c, 0), rows_of(k, c, 0), kx_s.at[k, d], kx_r.at[k, d], chip(d))
            go(("s", k, 0), rows_of(k, c, 0), rows_of(k, c, 0), ks_s.at[k, 0], ks_r.at[k, 0], sibling)

        for dy in (2, 1, 3):
            k = (-dy) % 4
            src = nrm.at[pl.ds(my_rows, OWN), chunk(dy)]
            go(("y", k), src, rows_of(k, c, 0), ky_s.at[k], ky_r.at[k], plane(dy, 0))
        rows_k[0, pl.ds(my_rows, OWN), :] = nrm[pl.ds(my_rows, OWN), chunk(0)]
        over_x(0)
        for k in (2, 1, 3):
            made["y", k].wait_recv()
            over_x(k)

        def ready(k):
            for d in (1, 3, 2):
                made["x", k, d].wait_recv()
                ref = rows_of(k, c, -d)
                go(("s", k, d), ref, ref, ks_s.at[k, d], ks_r.at[k, d], sibling)
            for d in (0, 1, 3, 2):
                made["s", k, d].wait_recv()

        def finish():
            for copy in made.values():
                copy.wait_send()

        return ready, finish

    def slice_gate_up(ready):
        made = []
        at = pl.ds(pl.multiple_of(y * SLICE, SLICE), SLICE)

        def product(k, mat):
            return jnp.dot(rows_k[k], full[mat][at, :], preferred_element_type=F32)

        def go(src, dst, send, recv, dy):
            copy = pltpu.make_async_remote_copy(
                src_ref=src, dst_ref=dst, send_sem=send, recv_sem=recv,
                device_id=plane(dy, 0), device_id_type=MESH,
            )
            copy.start()
            made.append(copy)
            return copy

        ready(2)
        far = []
        for mat in (0, 1):
            far_out[mat] = product(2, mat).astype(BF16)
            far.append(
                go(far_out.at[mat], far_in.at[mat], far_s.at[mat], far_r.at[mat], 1 - 2 * mat)
            )
        near = []

        def send_near(i, mat, value):
            near_out[i, mat] = value.astype(BF16)
            near.append(
                go(
                    near_out.at[i, mat], near_in.at[i, mat],
                    near_s.at[i, mat], near_r.at[i, mat], 1 - 2 * i,
                )
            )

        ready(1)
        send_near(0, 1, product(1, 1))
        ready(3)
        send_near(1, 0, product(3, 0))
        value = product(1, 0)
        far[0].wait_recv()
        send_near(0, 0, value + far_in[0].astype(F32))
        value = product(3, 1)
        far[1].wait_recv()
        send_near(1, 1, value + far_in[1].astype(F32))
        ready(0)
        for mat, acc in ((0, g_acc), (1, u_acc)):
            acc[...] = product(0, mat)

        def collect():
            for copy in near:
                copy.wait_recv()
            for mat, acc in ((0, g_acc), (1, u_acc)):
                acc[...] += near_in[0, mat].astype(F32) + near_in[1, mat].astype(F32)

        def finish():
            for copy in made:
                copy.wait_send()

        return collect, finish

    def attended(lo, hi):
        return att[lo // BLOCK : hi // BLOCK].reshape(hi - lo, HEADS * HEAD_DIM)

    def half_scatter(h, lhs, weight):
        rows = slice(64 * h, 64 * (h + 1))

        def to_sibling(n):
            return pltpu.make_async_remote_copy(
                src_ref=sib_out.at[n],
                dst_ref=sib_in.at[n],
                send_sem=sib_ss.at[n],
                recv_sem=sib_rs.at[n],
                device_id=sibling,
                device_id_type=MESH,
            )

        def to_chip(n, d):
            return pltpu.make_async_remote_copy(
                src_ref=x_out.at[n, add4(x, d)],
                dst_ref=x_in.at[n, d],
                send_sem=x_ss.at[n, d],
                recv_sem=x_rs.at[n, d],
                device_id=chip(d),
                device_id_type=MESH,
            )

        def chips(n):
            @pl.when(c == h)
            def _():
                to_sibling(n).wait_recv()
                total = part[n, rows, :] + sib_in[n].astype(F32)
                part[n, rows, :] = total
                x_out[n] = total.astype(BF16).reshape(4, OWN, RS_W)
                for d in (2, 1, 3):
                    to_chip(n, d).start()

        for n in range(N_RS):
            part[n, rows, :] = jnp.dot(
                lhs, weight[:, n * RS_W : (n + 1) * RS_W], preferred_element_type=F32
            )

            @pl.when(c != h)
            def _():
                sib_out[n] = part[n, rows, :].astype(BF16)
                to_sibling(n).start()

            if n > 0:
                chips(n - 1)
        chips(N_RS - 1)

        def own(n):
            total = part[n, pl.ds(my_rows, OWN), :]
            for d in (1, 3, 2):
                to_chip(n, d).wait_recv()
                total = total + x_in[n, d].astype(F32)
            return total

        def finish():
            @pl.when(c == h)
            def _():
                for n in range(N_RS):
                    for d in (1, 3, 2):
                        to_chip(n, d).wait_send()

            @pl.when(c != h)
            def _():
                for n in range(N_RS):
                    to_sibling(n).wait_send()

        return own, finish

    def half_rows(h, k, d):
        at = pl.ds(pl.multiple_of(64 * h + OWN * add4(x, -d), OWN), OWN)
        return nrm.at[at, pl.ds(k * AG_W, AG_W)]

    def row_copy(h, k, d, direct):
        ref = half_rows(h, k, 0 if direct else d)
        send, recv = (agx_s, agx_r) if direct else (ags_s, ags_r)
        return pltpu.make_async_remote_copy(
            src_ref=ref, dst_ref=ref, send_sem=send.at[k, d], recv_sem=recv.at[k, d],
            device_id=chip(d) if direct else sibling, device_id_type=MESH,
        )

    def half_finish(h, scattered, complete):
        own, finish = scattered

        @pl.when(c == h)
        def _():
            complete(own)
            for k in range(N_AG):
                for d in (2, 1, 3):
                    row_copy(h, k, d, True).start()
                row_copy(h, k, 0, False).start()

        finish()

    def half_ready(h):
        @pl.when(c == h)
        def _():
            for k in range(N_AG):
                for d in (1, 3, 2):
                    row_copy(h, k, d, True).wait_recv()
                    row_copy(h, k, d, False).start()

        @pl.when(c != h)
        def _():
            for k in range(N_AG):
                for d in (0, 1, 3, 2):
                    row_copy(h, k, d, False).wait_recv()

    def half_sent(h):
        @pl.when(c == h)
        def _():
            for k in range(N_AG):
                for d in (1, 3, 2):
                    row_copy(h, k, d, True).wait_send()
                for d in (0, 1, 3, 2):
                    row_copy(h, k, d, False).wait_send()

    def last_rows(own):
        for n in range(N_RS):
            cols = slice(n * RS_W, (n + 1) * RS_W)
            nrm[pl.ds(my_rows, OWN), cols] = (res[:, cols] + own(n)).astype(BF16)

    gather_0()
    tables()
    loads["blocks"].wait()
    norm_local()
    res[...] = x_v[pl.ds(my_rows, OWN), :].astype(F32)
    loads["wq"].wait()
    loads["wkv"].wait()
    project(0, ROWS)
    loads["prompt"].wait()
    loads["cache"].wait()
    attention(0, ROWS)
    loads["wo"].wait()
    own, rs_done = reduce_scatter(attended(0, ROWS), wo_v)
    turn(0, 0)
    turn(1, 1)
    turn(1, 0)
    turn(0, 1)
    after_attention(own, mlp_gain)
    rs_done()
    ready, rows_done = slice_rows()
    halves(0, 2, 0)
    halves(1, 0, 2)
    collect, sums_done = slice_gate_up(ready)
    halves(1, 2, 0)
    for a in (-1, 1, 2):
        spread(1, a)
    collect()
    for a in (-1, 1, 2):
        spread(0, a)
    rows_done()
    sums_done()
    activate(0, ROWS)
    loads["wd"].wait()
    loads["tok"].wait()
    low, high = (0, 64), (64, 128)
    sums_0 = half_scatter(0, hid[:64, :], wd_v)
    sums_1 = half_scatter(1, hid[64:, :], wd_v)

    half_finish(0, sums_0, between_passes)
    half_finish(1, sums_1, between_passes)
    half_ready(0)
    project(*low)
    half_sent(0)
    attention(*low)
    sums_0 = half_scatter(0, attended(*low), wo_v)
    half_ready(1)
    project(*high)
    half_sent(1)
    for a in (-1, 1, 2):
        forward(1, a)
    attention(*high)
    half_finish(0, sums_0, lambda own: after_attention(own, mlp_gain))
    sums_1 = half_scatter(1, attended(*high), wo_v)
    for a in (-1, 1, 2):
        forward(0, a)
    half_ready(0)
    halves(0, 0, 2)
    for a in (-1, 1, 2):
        halves(0, a, 2)
        halves(1, a, 2)
    gate_up(*low)
    half_sent(0)
    half_finish(1, sums_1, lambda own: after_attention(own, mlp_gain))
    sums_0 = half_scatter(0, hid[:64, :], wd_v)
    half_ready(1)
    gate_up(*high)
    half_sent(1)
    half_finish(0, sums_0, last_rows)
    sums_1 = half_scatter(1, hid[64:, :], wd_v)
    half_finish(1, sums_1, last_rows)
    half_ready(0)
    half_ready(1)
    half_sent(0)
    half_sent(1)
    for copy in sends[0] + sends[1]:
        copy.wait_send()
    copy = pltpu.make_async_copy(nrm, out, load_sem.at[0])
    copy.start()
    copy.wait()


def body(
    blocks, token_embed, accepted, prompt_len, cache_len, prompt_kv, cache_kv, attn_gain,
    w_q, w_kv, w_o, mlp_gain, w_gate, w_up, w_down,
):
    half = np.arange(HEAD_DIM // 2, dtype=np.float32)
    frequency = np.float32(THETA) ** (np.float32(-2.0) * half / np.float32(HEAD_DIM))
    frequency = jnp.asarray(np.concatenate([frequency, frequency])[None, :], dtype=F32)

    vmem = pl.BlockSpec(memory_space=pltpu.VMEM)
    anywhere = pl.BlockSpec(memory_space=pl.ANY)
    dma = pltpu.SemaphoreType.DMA
    return pl.pallas_call(
        kernel,
        out_shape=jax.ShapeDtypeStruct((ROWS, D), BF16),
        in_specs=[pl.BlockSpec(memory_space=pltpu.SMEM)] * 2 + [vmem] * 4 + [anywhere] * 10,
        out_specs=anywhere,
        scratch_shapes=[
            pltpu.VMEM((ROWS, D), BF16),
            pltpu.VMEM((OWN, D), BF16),
            pltpu.VMEM((PMAX, 2 * HEAD_DIM), BF16),
            pltpu.VMEM((REQS, CACHE, 2 * HEAD_DIM), BF16),
            pltpu.VMEM((D, HEADS * HEAD_DIM), BF16),
            pltpu.VMEM((D, 2 * HEAD_DIM), BF16),
            pltpu.VMEM((HEADS * HEAD_DIM, D), BF16),
            pltpu.VMEM((D, HIDDEN), BF16),
            pltpu.VMEM((D, HIDDEN), BF16),
            pltpu.VMEM((HIDDEN, D), BF16),
            pltpu.VMEM((ROWS, D), BF16),
            pltpu.VMEM((ROWS, (HEADS + 2) * HEAD_DIM), F32),
            pltpu.VMEM((REQS, HEADS * BLOCK, HEAD_DIM), BF16),
            pltpu.VMEM((REQS, BLOCK, HEAD_DIM), BF16),
            pltpu.VMEM((REQS, BLOCK, HEAD_DIM), BF16),
            pltpu.VMEM((REQS, BLOCK, HEADS * HEAD_DIM), BF16),
            pltpu.VMEM((ROWS, HIDDEN), F32),
            pltpu.VMEM((ROWS, HIDDEN), F32),
            pltpu.VMEM((ROWS, HIDDEN), BF16),
            pltpu.VMEM((N_RS, ROWS, RS_W), F32),
            pltpu.VMEM((N_RS, 64, RS_W), BF16),
            pltpu.VMEM((N_RS, 64, RS_W), BF16),
            pltpu.VMEM((N_RS, 4, OWN, RS_W), BF16),
            pltpu.VMEM((N_RS, 4, OWN, RS_W), BF16),
            pltpu.VMEM((OWN, D), F32),
            pltpu.VMEM((ROWS, HEAD_DIM), F32),
            pltpu.VMEM((ROWS, HEAD_DIM), F32),
            pltpu.VMEM((4, ROWS, SLICE), BF16),
            pltpu.VMEM((2, ROWS, HIDDEN), BF16),
            pltpu.VMEM((2, ROWS, HIDDEN), BF16),
            pltpu.VMEM((2, 2, ROWS, HIDDEN), BF16),
            pltpu.VMEM((2, 2, ROWS, HIDDEN), BF16),
            dma((10,)),
            dma((2, 20)),
            dma((2, 4, 4, 2)),
            dma((N_RS,)),
            dma((N_RS,)),
            dma((N_RS, 4)),
            dma((N_RS, 4)),
            dma((N_AG, 4)),
            dma((N_AG, 4)),
            dma((N_AG, 4)),
            dma((N_AG, 4)),
            dma((4,)),
            dma((4,)),
            dma((4, 4)),
            dma((4, 4)),
            dma((4, 4)),
            dma((4, 4)),
            dma((2,)),
            dma((2,)),
            dma((2, 2)),
            dma((2, 2)),
        ],
        compiler_params=pltpu.CompilerParams(
            collective_id=0, has_side_effects=True, vmem_limit_bytes=60 * 2**20
        ),
        name="two_passes",
    )(
        prompt_len, cache_len, accepted[None, :], frequency, attn_gain[None, :], mlp_gain[None, :],
        blocks, token_embed, prompt_kv[0], cache_kv[0], w_q, w_kv, w_o, w_gate, w_up, w_down,
    )


def solution(mesh):
    return jax.shard_map(
        body,
        mesh=mesh,
        in_specs=(
            P("req", None),
            P("req", None),
            P("req"),
            P("req"),
            P("req", None),
            P("req", None, "mlp"),
            P("req", None, None, "mlp"),
            P(),
            P(None, "mlp"),
            P(None, "mlp"),
            P("mlp", None),
            P(),
            P("req", "mlp"),
            P("req", "mlp"),
            P("mlp", None),
        ),
        out_specs=P("req", None),
        check_vma=False,
    )
```

```python
import math

import jax
import jax.numpy as jnp
from jax import lax
from jax.experimental import pallas as pl
from jax.experimental.pallas import tpu as pltpu
from jax.sharding import PartitionSpec as P
import numpy as np

D = 4096
HEAD_DIM = 128
HEADS = 4
REQS = 8
BLOCK = 16
ROWS = REQS * BLOCK
CACHE = 1024
PMAX = 512
HIDDEN = 896
SHARD = 256
SLICE = 1024
OWN = 16
EPSILON = 1e-05
THETA = 500000.0
MESH = pl.DeviceIdType.MESH
N_RS = 4
RS_W = D // N_RS
N_AG = 2
AG_W = D // N_AG
F32 = jnp.float32
BF16 = jnp.bfloat16


def kernel(
    prompt_len, cache_len, accepted, frequency, attn_gain, mlp_gain,
    blocks, token, prompt, cache, w_q, w_kv, w_o, w_gate, w_up, w_down,
    out,
    x_v, tok_v, prm_v, cache_v, wq_v, wkv_v, wo_v, gate_v, up_v, wd_v,
    nrm, qkv, q_s, k_s, v_s, att, g_acc, u_acc, hid,
    part, sib_out, sib_in, x_out, x_in, res, cos, sin,
    strided, rows_k, far_out, far_in, near_keep, near_out, near_in,
    load_sem, g_send, g_recv, sib_ss, sib_rs, x_ss, x_rs, agx_s, agx_r, ags_s, ags_r,
    ky_s, ky_r, kx_s, kx_r, ks_s, ks_r, far_s, far_r, near_s, near_r,
):
    r = lax.axis_index("req")
    m = lax.axis_index("mlp")
    y, z = lax.div(r, 4), lax.rem(r, 4)
    x, c = lax.div(m, 2), lax.rem(m, 2)

    def add4(v, d):
        return lax.rem(v + (d % 4), 4)

    def chip(d):
        return (r, add4(x, d) * 2 + c)

    sibling = (r, x * 2 + 1 - c)

    def plane(dy, dz):
        return (add4(y, dy) * 4 + add4(z, dz), m)

    my_half = pl.multiple_of(64 * c, 64)
    other_half = pl.multiple_of(64 * (1 - c), 64)
    my_rows = pl.multiple_of(64 * c + OWN * x, OWN)

    own_shard = pl.ds(pl.multiple_of(r * SHARD, SHARD), SHARD)
    loads = {}
    for i, (name, src, dst) in enumerate(
        [
            ("gate", w_gate, gate_v.at[own_shard]),
            ("up", w_up, up_v.at[own_shard]),
            ("blocks", blocks, x_v),
            ("wq", w_q, wq_v),
            ("wkv", w_kv, wkv_v),
            ("prompt", prompt, prm_v),
            ("cache", cache, cache_v),
            ("wo", w_o, wo_v),
            ("wd", w_down, wd_v),
            ("tok", token.at[pl.ds(my_rows, OWN)], tok_v),
        ]
    ):
        copy = pltpu.make_async_copy(src, dst, load_sem.at[i])
        copy.start()
        loads[name] = copy

    barrier = pltpu.get_barrier_semaphore()
    partners = [chip(1), chip(2), chip(3), sibling, plane(0, 1), plane(0, 3), plane(1, 0), plane(3, 0), plane(2, 0), plane(0, 2)]
    for who in partners:
        pl.semaphore_signal(barrier, inc=1, device_id=who, device_id_type=MESH)
    pl.semaphore_wait(barrier, len(partners))

    full = (gate_v, up_v)
    sends = ([], [])

    def index(mat, a, b):
        dy, dz = (b, a) if mat == 0 else (a, b)
        return add4(y, dy) * 4 + add4(z, dz)

    def piece(mat, a, b, half):
        start = index(mat, a, b) * SHARD
        if half is None:
            return full[mat].at[pl.ds(pl.multiple_of(start, SHARD), SHARD)]
        return full[mat].at[pl.ds(pl.multiple_of(start + half * (SHARD // 2), SHARD // 2), SHARD // 2)]

    def g_copy(mat, a, b, half, axis, step, send_sem):
        da, db = (step, 0) if axis == 0 else (0, step)
        dy, dz = (db, da) if mat == 0 else (da, db)
        ref = piece(mat, a, b, half)
        return pltpu.make_async_remote_copy(
            src_ref=ref,
            dst_ref=ref,
            send_sem=send_sem,
            recv_sem=g_recv.at[mat, (a - da) % 4, (b - db) % 4, half or 0],
            device_id=plane(dy, dz),
            device_id_type=MESH,
        )

    def g_start(mat, a, b, half, axis, step):
        copy = g_copy(mat, a, b, half, axis, step, g_send.at[mat, len(sends[mat])])
        copy.start()
        sends[mat].append(copy)

    def g_wait(mat, a, b, half=None):
        ref = piece(mat, a, b, half)
        pltpu.make_async_remote_copy(
            src_ref=ref,
            dst_ref=ref,
            send_sem=g_send.at[mat, 0],
            recv_sem=g_recv.at[mat, a % 4, b % 4, half or 0],
            device_id=plane(0, 1),
            device_id_type=MESH,
        ).wait_recv()

    def gather_0():
        for mat, name in ((0, "gate"), (1, "up")):
            loads[name].wait()
            g_start(mat, 0, 0, None, 0, 1)
            g_start(mat, 0, 0, None, 0, -1)

    def turn(mat, axis):
        for step, half in ((1, 0), (-1, 1)):
            at = (-step, 0) if axis == 0 else (0, -step)
            g_wait(mat, *at)
            g_start(mat, *at, half, axis, step)

    def spread(mat, a):
        g_start(mat, a, 0, None, 1, 1)
        g_start(mat, a, 0, None, 1, -1)

    def halves(mat, a, b):
        g_wait(mat, a, b, 0)
        g_wait(mat, a, b, 1)

    def forward(mat, a):
        g_wait(mat, a, -1)
        g_start(mat, a, -1, 0, 1, 1)
        g_wait(mat, a, 1)
        g_start(mat, a, 1, 1, 1, -1)

    def tables():
        lane = lax.broadcasted_iota(jnp.int32, (BLOCK, HEAD_DIM), 1)
        row = lax.broadcasted_iota(jnp.int32, (BLOCK, HEAD_DIM), 0)
        for j in range(REQS):
            position = row + (prompt_len[0] + cache_len[0, j])
            angle = position.astype(F32) * frequency[...]
            cos[BLOCK * j : BLOCK * (j + 1), :] = jnp.cos(angle)
            sine = jnp.sin(angle)
            sin[BLOCK * j : BLOCK * (j + 1), :] = jnp.where(lane < HEAD_DIM // 2, -sine, sine)

    def norm_local():
        def step(i, carry):
            rows = pl.ds(pl.multiple_of(i * OWN, OWN), OWN)
            wide = x_v[rows, :].astype(F32)
            scale = lax.rsqrt(jnp.mean(wide * wide, axis=-1, keepdims=True) + EPSILON)
            nrm[rows, :] = (wide * scale * attn_gain[...]).astype(BF16)
            return carry

        lax.fori_loop(0, ROWS // OWN, step, 0)

    def project(ready):
        for k in range(N_AG):
            ready(k)
            cols = slice(k * AG_W, (k + 1) * AG_W)
            lhs = nrm[:, cols]
            q_part = jnp.dot(lhs, wq_v[cols, :], preferred_element_type=F32)
            kv_part = jnp.dot(lhs, wkv_v[cols, :], preferred_element_type=F32)
            if k == 0:
                qkv[:, : HEADS * HEAD_DIM] = q_part
                qkv[:, HEADS * HEAD_DIM :] = kv_part
            else:
                qkv[:, : HEADS * HEAD_DIM] += q_part
                qkv[:, HEADS * HEAD_DIM :] += kv_part

    def attention():
        def rope(values):
            return (values * cos[...] + pltpu.roll(values, HEAD_DIM // 2, 1) * sin[...]).astype(BF16)

        for h in range(HEADS):
            q_s[:, BLOCK * h : BLOCK * (h + 1), :] = rope(
                qkv[:, HEAD_DIM * h : HEAD_DIM * (h + 1)]
            ).reshape(REQS, BLOCK, HEAD_DIM)
        base = HEADS * HEAD_DIM
        k_s[...] = rope(qkv[:, base : base + HEAD_DIM]).reshape(REQS, BLOCK, HEAD_DIM)
        v_s[...] = qkv[:, base + HEAD_DIM :].astype(BF16).reshape(REQS, BLOCK, HEAD_DIM)
        scale = math.log2(math.e) / math.sqrt(HEAD_DIM)
        contract = (((1,), (1,)), ((), ()))

        def step(j, carry):
            q = q_s[j]

            def scores(keys):
                return lax.dot_general(q, keys, contract, preferred_element_type=F32) * scale

            s_c = scores(cache_v[j, :, :HEAD_DIM])
            s_p = scores(prm_v[:, :HEAD_DIM])
            s_b = scores(k_s[j])
            at_c = lax.broadcasted_iota(jnp.int32, s_c.shape, 1)
            at_p = lax.broadcasted_iota(jnp.int32, s_p.shape, 1)
            s_c = jnp.where(at_c < cache_len[0, j], s_c, -1e30)
            s_p = jnp.where(at_p < prompt_len[0], s_p, -1e30)
            top = jnp.maximum(
                jnp.maximum(jnp.max(s_c, -1, keepdims=True), jnp.max(s_p, -1, keepdims=True)),
                jnp.max(s_b, -1, keepdims=True),
            )
            e_c = jnp.exp2(s_c - top)
            e_p = jnp.exp2(s_p - top)
            e_b = jnp.exp2(s_b - top)
            total = (
                jnp.sum(e_c, -1, keepdims=True)
                + jnp.sum(e_p, -1, keepdims=True)
                + jnp.sum(e_b, -1, keepdims=True)
            )
            mixed = jnp.dot(e_c.astype(BF16), cache_v[j, :, HEAD_DIM:], preferred_element_type=F32)
            mixed += jnp.dot(e_p.astype(BF16), prm_v[:, HEAD_DIM:], preferred_element_type=F32)
            mixed += jnp.dot(e_b.astype(BF16), v_s[j], preferred_element_type=F32)
            mixed = (mixed / total).astype(BF16)
            for h in range(HEADS):
                att[j, :, HEAD_DIM * h : HEAD_DIM * (h + 1)] = mixed[BLOCK * h : BLOCK * (h + 1)]
            return carry

        lax.fori_loop(0, REQS, step, 0, unroll=2)

    pending = []

    def reduce_scatter(lhs, weight):
        def chips(n):
            sib_copies[n].wait_recv()
            total = part[n, pl.ds(my_half, 64), :] + sib_in[n].astype(F32)
            part[n, pl.ds(my_half, 64), :] = total
            x_out[n] = total.astype(BF16).reshape(4, OWN, RS_W)
            for d in (2, 1, 3):
                copy = pltpu.make_async_remote_copy(
                    src_ref=x_out.at[n, add4(x, d)],
                    dst_ref=x_in.at[n, d],
                    send_sem=x_ss.at[n, d],
                    recv_sem=x_rs.at[n, d],
                    device_id=chip(d),
                    device_id_type=MESH,
                )
                copy.start()
                x_copies.append(copy)

        sib_copies, x_copies = [], []
        for n in range(N_RS):
            part[n] = jnp.dot(lhs, weight[:, n * RS_W : (n + 1) * RS_W], preferred_element_type=F32)
            sib_out[n] = part[n, pl.ds(other_half, 64), :].astype(BF16)
            copy = pltpu.make_async_remote_copy(
                src_ref=sib_out.at[n],
                dst_ref=sib_in.at[n],
                send_sem=sib_ss.at[n],
                recv_sem=sib_rs.at[n],
                device_id=sibling,
                device_id_type=MESH,
            )
            copy.start()
            sib_copies.append(copy)
            if n > 0:
                chips(n - 1)
        chips(N_RS - 1)

        def own(n):
            total = part[n, pl.ds(my_rows, OWN), :]
            for i, d in enumerate((2, 1, 3)):
                x_copies[3 * n + i].wait_recv()
                total = total + x_in[n, d].astype(F32)
            return total

        def finish():
            for copy in sib_copies + x_copies:
                copy.wait_send()

        return own, finish

    def normalize(square_sum, gain):
        scale = lax.rsqrt(square_sum / D + EPSILON)
        for n in range(N_RS):
            cols = slice(n * RS_W, (n + 1) * RS_W)
            nrm[pl.ds(my_rows, OWN), cols] = (res[:, cols] * scale * gain[:, cols]).astype(BF16)

    def share_rows():
        ag = {}

        def copy_rows(k, row, send, recv, who):
            ref = nrm.at[pl.ds(pl.multiple_of(row, OWN), OWN), pl.ds(k * AG_W, AG_W)]
            return pltpu.make_async_remote_copy(
                src_ref=ref, dst_ref=ref, send_sem=send, recv_sem=recv, device_id=who, device_id_type=MESH
            )

        for k in range(N_AG):
            for d in (2, 1, 3):
                ag[k, d] = copy_rows(k, my_rows, agx_s.at[k, d], agx_r.at[k, d], chip(d))
                ag[k, d].start()
            ag[k, 4] = copy_rows(k, my_rows, ags_s.at[k, 0], ags_r.at[k, 0], sibling)
            ag[k, 4].start()

        def ready(k):
            for d in (1, 3, 2):
                row = 64 * c + OWN * add4(x, -d)
                copy_rows(k, row, agx_s.at[k, d], agx_r.at[k, d], sibling).wait_recv()
                ag[k, 4 + d] = copy_rows(k, row, ags_s.at[k, d], ags_r.at[k, d], sibling)
                ag[k, 4 + d].start()
            for d in (0, 1, 3, 2):
                row = 64 * (1 - c) + OWN * add4(x, -d)
                copy_rows(k, row, ags_s.at[k, d], ags_r.at[k, d], sibling).wait_recv()

        def finish():
            for copy in ag.values():
                copy.wait_send()

        return ready, finish

    def after_attention(own, gain):
        square_sum = jnp.zeros((OWN, 1), F32)
        for n in range(N_RS):
            cols = slice(n * RS_W, (n + 1) * RS_W)
            total = (res[:, cols] + own(n)).astype(BF16).astype(F32)
            res[:, cols] = total
            square_sum += jnp.sum(total * total, axis=-1, keepdims=True)
        normalize(square_sum, gain)

    def between_passes(own):
        lane = lax.broadcasted_iota(jnp.int32, (OWN, ROWS), 1)
        row = lax.broadcasted_iota(jnp.int32, (OWN, ROWS), 0) + my_rows
        mine = jnp.where(lane == row, accepted[...].astype(F32), 0.0)
        take = jnp.sum(mine, axis=-1, keepdims=True) == 1.0
        square_sum = jnp.zeros((OWN, 1), F32)
        for n in range(N_RS):
            cols = slice(n * RS_W, (n + 1) * RS_W)
            first = (res[:, cols] + own(n)).astype(BF16).astype(F32)
            total = jnp.where(take, tok_v[:, cols].astype(F32), first)
            res[:, cols] = total
            square_sum += jnp.sum(total * total, axis=-1, keepdims=True)
        normalize(square_sum, attn_gain)

    def activate():
        gate = g_acc[...]
        hid[...] = (gate / (1.0 + jnp.exp(-gate)) * u_acc[...]).astype(BF16)

    def along(mat, d):
        return plane(d, 0) if mat == 0 else plane(0, d)

    def slice_rows():
        made = {}

        def go(key, src, dst, send, recv, who):
            made[key] = pltpu.make_async_remote_copy(
                src_ref=src, dst_ref=dst, send_sem=send, recv_sem=recv, device_id=who, device_id_type=MESH
            )
            made[key].start()

        def rows_of(mat, k, core, d):
            row = 64 * core + OWN * add4(x, d)
            return rows_k.at[mat, k, pl.ds(pl.multiple_of(row, OWN), OWN)]

        def chunk(mat, d):
            if mat == 0:
                at = pl.ds(pl.multiple_of(add4(y, d) * SLICE, SLICE), SLICE)
                return nrm.at[pl.ds(my_rows, OWN), at]
            return strided.at[add4(z, d)]

        def over_x(mat, k):
            ref = rows_of(mat, k, c, 0)
            for d in (2, 1, 3):
                go(("x", mat, k, d), ref, ref, kx_s.at[mat, k, d], kx_r.at[mat, k, d], chip(d))
            go(("s", mat, k, 0), ref, ref, ks_s.at[mat, k, 0], ks_r.at[mat, k, 0], sibling)

        for i in range(4):
            for j in range(4):
                start = SLICE * j + SHARD * i
                strided[i, :, SHARD * j : SHARD * (j + 1)] = nrm[
                    pl.ds(my_rows, OWN), start : start + SHARD
                ]
        for d in (2, 1, 3):
            for mat in (0, 1):
                k = (-d) % 4
                go(
                    ("p", mat, k), chunk(mat, d), rows_of(mat, k, c, 0),
                    ky_s.at[mat, k], ky_r.at[mat, k], along(mat, d),
                )
        for mat in (0, 1):
            rows_k[mat, 0, pl.ds(my_rows, OWN), :] = chunk(mat, 0)[...]
        for k in (2, 1, 3, 0):
            for mat in (0, 1):
                if k > 0:
                    made["p", mat, k].wait_recv()
                over_x(mat, k)

        def ready(mat, k):
            for d in (1, 3, 2):
                made["x", mat, k, d].wait_recv()
                ref = rows_of(mat, k, c, -d)
                go(("s", mat, k, d), ref, ref, ks_s.at[mat, k, d], ks_r.at[mat, k, d], sibling)
            for d in (0, 1, 3, 2):
                made["s", mat, k, d].wait_recv()

        def finish():
            for copy in made.values():
                copy.wait_send()

        return ready, finish

    def slice_gate_up(ready):
        made = []
        accs = (g_acc, u_acc)
        half = ROWS // 2

        def product(mat, k):
            if mat == 0:
                at = pl.ds(pl.multiple_of(y * SLICE, SLICE), SLICE)
                return jnp.dot(rows_k[0, k], gate_v[at, :], preferred_element_type=F32)
            total = jnp.zeros((ROWS, HIDDEN), F32)
            for j in range(4):
                at = pl.ds(pl.multiple_of((4 * j + z) * SHARD, SHARD), SHARD)
                lhs = rows_k[1, k, :, SHARD * j : SHARD * (j + 1)]
                total += jnp.dot(lhs, up_v[at, :], preferred_element_type=F32)
            return total

        def go(src, dst, send, recv, who):
            copy = pltpu.make_async_remote_copy(
                src_ref=src, dst_ref=dst, send_sem=send, recv_sem=recv, device_id=who, device_id_type=MESH
            )
            copy.start()
            made.append(copy)
            return copy

        far = {}
        for mat in (0, 1):
            ready(mat, 2)
            value = product(mat, 2).astype(BF16)
            for i in (0, 1):
                far_out[mat, i] = value[half * i : half * (i + 1)]
                far[mat, i] = go(
                    far_out.at[mat, i], far_in.at[mat, i], far_s.at[mat, i], far_r.at[mat, i],
                    along(mat, 1 - 2 * i),
                )
        near = []

        def send_near(i, mat, part_i):
            near.append(
                go(
                    near_out.at[i, mat, part_i], near_in.at[i, mat, part_i],
                    near_s.at[i, mat, part_i], near_r.at[i, mat, part_i], along(mat, 1 - 2 * i),
                )
            )

        for i in (0, 1):
            for mat in (0, 1):
                ready(mat, 1 + 2 * i)
                value = product(mat, 1 + 2 * i)
                near_keep[i, mat] = value[half * i : half * (i + 1)]
                near_out[i, mat, 1 - i] = value[half * (1 - i) : half * (2 - i)].astype(BF16)
                send_near(i, mat, 1 - i)
        for i in (0, 1):
            for mat in (0, 1):
                far[mat, i].wait_recv()
                near_out[i, mat, i] = (near_keep[i, mat] + far_in[mat, i].astype(F32)).astype(BF16)
                send_near(i, mat, i)
        for mat in (0, 1):
            ready(mat, 0)
            accs[mat][...] = product(mat, 0)

        def collect():
            for copy in near:
                copy.wait_recv()
            for mat in (0, 1):
                for i in (0, 1):
                    rows = slice(half * i, half * (i + 1))
                    accs[mat][rows, :] += near_in[0, mat, i].astype(F32) + near_in[1, mat, i].astype(F32)

        def finish():
            for copy in made:
                copy.wait_send()

        return collect, finish

    def attended():
        return att[...].reshape(ROWS, HEADS * HEAD_DIM)

    gather_0()
    tables()
    loads["blocks"].wait()
    norm_local()
    res[...] = x_v[pl.ds(my_rows, OWN), :].astype(F32)
    loads["wq"].wait()
    loads["wkv"].wait()
    project(lambda k: None)
    loads["prompt"].wait()
    loads["cache"].wait()
    attention()
    for mat in (0, 1):
        turn(mat, 0)
    for mat in (0, 1):
        g_start(mat, 0, 0, None, 1, 1)
        g_start(mat, 0, 0, None, 1, -1)
    loads["wo"].wait()
    own, rs_done = reduce_scatter(attended(), wo_v)
    after_attention(own, mlp_gain)
    rs_done()
    ready, rows_done = slice_rows()
    halves(0, 2, 0)
    halves(1, 2, 0)
    collect, sums_done = slice_gate_up(ready)
    for mat in (0, 1):
        turn(mat, 1)
    collect()
    for a in (-1, 1, 2):
        for mat in (0, 1):
            spread(mat, a)
    rows_done()
    sums_done()
    activate()
    loads["wd"].wait()
    loads["tok"].wait()
    own, rs_done = reduce_scatter(hid[...], wd_v)
    between_passes(own)
    rs_done()

    ready, ag_done = share_rows()
    project(ready)
    ag_done()
    for a in (-1, 1):
        for mat in (0, 1):
            forward(mat, a)
    attention()
    own, rs_done = reduce_scatter(attended(), wo_v)
    for mat in (0, 1):
        forward(mat, 2)
    after_attention(own, mlp_gain)
    rs_done()
    ready, ag_done = share_rows()
    for a in (0, -1, 1, 2):
        halves(0, a, 2)
        halves(1, a, 2)
    for k in range(N_AG):
        ready(k)
        for part_k in range(2):
            start = k * AG_W + part_k * (AG_W // 2)
            at = slice(start, start + AG_W // 2)
            for acc, weight in ((g_acc, gate_v), (u_acc, up_v)):
                product = jnp.dot(nrm[:, at], weight[at, :], preferred_element_type=F32)
                if start == 0:
                    acc[...] = product
                else:
                    acc[...] += product
    ag_done()
    for copy in sends[0] + sends[1]:
        copy.wait_send()
    activate()
    own, rs_done = reduce_scatter(hid[...], wd_v)
    for n in range(N_RS):
        cols = slice(n * RS_W, (n + 1) * RS_W)
        nrm[pl.ds(my_rows, OWN), cols] = (res[:, cols] + own(n)).astype(BF16)
    rs_done()
    ready, ag_done = share_rows()
    for k in range(N_AG):
        ready(k)
    ag_done()
    copy = pltpu.make_async_copy(nrm, out, load_sem.at[0])
    copy.start()
    copy.wait()


def body(
    blocks, token_embed, accepted, prompt_len, cache_len, prompt_kv, cache_kv, attn_gain,
    w_q, w_kv, w_o, mlp_gain, w_gate, w_up, w_down,
):
    half = np.arange(HEAD_DIM // 2, dtype=np.float32)
    frequency = np.float32(THETA) ** (np.float32(-2.0) * half / np.float32(HEAD_DIM))
    frequency = jnp.asarray(np.concatenate([frequency, frequency])[None, :], dtype=F32)

    vmem = pl.BlockSpec(memory_space=pltpu.VMEM)
    anywhere = pl.BlockSpec(memory_space=pl.ANY)
    dma = pltpu.SemaphoreType.DMA
    return pl.pallas_call(
        kernel,
        out_shape=jax.ShapeDtypeStruct((ROWS, D), BF16),
        in_specs=[pl.BlockSpec(memory_space=pltpu.SMEM)] * 2 + [vmem] * 4 + [anywhere] * 10,
        out_specs=anywhere,
        scratch_shapes=[
            pltpu.VMEM((ROWS, D), BF16),
            pltpu.VMEM((OWN, D), BF16),
            pltpu.VMEM((PMAX, 2 * HEAD_DIM), BF16),
            pltpu.VMEM((REQS, CACHE, 2 * HEAD_DIM), BF16),
            pltpu.VMEM((D, HEADS * HEAD_DIM), BF16),
            pltpu.VMEM((D, 2 * HEAD_DIM), BF16),
            pltpu.VMEM((HEADS * HEAD_DIM, D), BF16),
            pltpu.VMEM((D, HIDDEN), BF16),
            pltpu.VMEM((D, HIDDEN), BF16),
            pltpu.VMEM((HIDDEN, D), BF16),
            pltpu.VMEM((ROWS, D), BF16),
            pltpu.VMEM((ROWS, (HEADS + 2) * HEAD_DIM), F32),
            pltpu.VMEM((REQS, HEADS * BLOCK, HEAD_DIM), BF16),
            pltpu.VMEM((REQS, BLOCK, HEAD_DIM), BF16),
            pltpu.VMEM((REQS, BLOCK, HEAD_DIM), BF16),
            pltpu.VMEM((REQS, BLOCK, HEADS * HEAD_DIM), BF16),
            pltpu.VMEM((ROWS, HIDDEN), F32),
            pltpu.VMEM((ROWS, HIDDEN), F32),
            pltpu.VMEM((ROWS, HIDDEN), BF16),
            pltpu.VMEM((N_RS, ROWS, RS_W), F32),
            pltpu.VMEM((N_RS, 64, RS_W), BF16),
            pltpu.VMEM((N_RS, 64, RS_W), BF16),
            pltpu.VMEM((N_RS, 4, OWN, RS_W), BF16),
            pltpu.VMEM((N_RS, 4, OWN, RS_W), BF16),
            pltpu.VMEM((OWN, D), F32),
            pltpu.VMEM((ROWS, HEAD_DIM), F32),
            pltpu.VMEM((ROWS, HEAD_DIM), F32),
            pltpu.VMEM((4, OWN, SLICE), BF16),
            pltpu.VMEM((2, 4, ROWS, SLICE), BF16),
            pltpu.VMEM((2, 2, ROWS // 2, HIDDEN), BF16),
            pltpu.VMEM((2, 2, ROWS // 2, HIDDEN), BF16),
            pltpu.VMEM((2, 2, ROWS // 2, HIDDEN), F32),
            pltpu.VMEM((2, 2, 2, ROWS // 2, HIDDEN), BF16),
            pltpu.VMEM((2, 2, 2, ROWS // 2, HIDDEN), BF16),
            dma((10,)),
            dma((2, 20)),
            dma((2, 4, 4, 2)),
            dma((N_RS,)),
            dma((N_RS,)),
            dma((N_RS, 4)),
            dma((N_RS, 4)),
            dma((N_AG, 4)),
            dma((N_AG, 4)),
            dma((N_AG, 4)),
            dma((N_AG, 4)),
            dma((2, 4)),
            dma((2, 4)),
            dma((2, 4, 4)),
            dma((2, 4, 4)),
            dma((2, 4, 4)),
            dma((2, 4, 4)),
            dma((2, 2)),
            dma((2, 2)),
            dma((2, 2, 2)),
            dma((2, 2, 2)),
        ],
        compiler_params=pltpu.CompilerParams(
            collective_id=0, has_side_effects=True, vmem_limit_bytes=60 * 2**20
        ),
        name="two_passes",
    )(
        prompt_len, cache_len, accepted[None, :], frequency, attn_gain[None, :], mlp_gain[None, :],
        blocks, token_embed, prompt_kv[0], cache_kv[0], w_q, w_kv, w_o, w_gate, w_up, w_down,
    )


def solution(mesh):
    return jax.shard_map(
        body,
        mesh=mesh,
        in_specs=(
            P("req", None),
            P("req", None),
            P("req"),
            P("req"),
            P("req", None),
            P("req", None, "mlp"),
            P("req", None, None, "mlp"),
            P(),
            P(None, "mlp"),
            P(None, "mlp"),
            P("mlp", None),
            P(),
            P("req", "mlp"),
            P("req", "mlp"),
            P("mlp", None),
        ),
        out_specs=P("req", None),
        check_vma=False,
    )
```

```python
import math

import jax
import jax.numpy as jnp
from jax import lax
from jax.experimental import pallas as pl
from jax.experimental.pallas import tpu as pltpu
from jax.sharding import PartitionSpec as P
import numpy as np

D = 4096
HEAD_DIM = 128
HEADS = 4
REQS = 8
BLOCK = 16
ROWS = REQS * BLOCK
CACHE = 1024
PMAX = 512
HIDDEN = 896
SHARD = 256
SLICE = 1024
OWN = 16
EPSILON = 1e-05
THETA = 500000.0
MESH = pl.DeviceIdType.MESH
N_RS = 4
RS_W = D // N_RS
N_AG = 2
AG_W = D // N_AG
F32 = jnp.float32
BF16 = jnp.bfloat16


def kernel(
    prompt_len, cache_len, accepted, frequency, attn_gain, mlp_gain,
    blocks, token, prompt, cache, w_q, w_kv, w_o, w_gate, w_up, w_down,
    out,
    x_v, tok_v, prm_v, cache_v, wq_v, wkv_v, wo_v, gate_v, up_v, wd_v,
    nrm, qkv, q_s, k_s, v_s, att, g_acc, u_acc, hid,
    part, sib_out, sib_in, x_out, x_in, res, cos, sin,
    strided, rows_k, far_out, far_in, near_keep, near_out, near_in,
    load_sem, g_send, g_recv, sib_ss, sib_rs, x_ss, x_rs, agx_s, agx_r, ags_s, ags_r,
    ky_s, ky_r, kx_s, kx_r, ks_s, ks_r, far_s, far_r, near_s, near_r,
):
    r = lax.axis_index("req")
    m = lax.axis_index("mlp")
    y, z = lax.div(r, 4), lax.rem(r, 4)
    x, c = lax.div(m, 2), lax.rem(m, 2)

    def add4(v, d):
        return lax.rem(v + (d % 4), 4)

    def chip(d):
        return (r, add4(x, d) * 2 + c)

    sibling = (r, x * 2 + 1 - c)

    def plane(dy, dz):
        return (add4(y, dy) * 4 + add4(z, dz), m)

    my_half = pl.multiple_of(64 * c, 64)
    other_half = pl.multiple_of(64 * (1 - c), 64)
    my_rows = pl.multiple_of(64 * c + OWN * x, OWN)

    own_shard = pl.ds(pl.multiple_of(r * SHARD, SHARD), SHARD)
    loads = {}
    for i, (name, src, dst) in enumerate(
        [
            ("gate", w_gate, gate_v.at[own_shard]),
            ("up", w_up, up_v.at[own_shard]),
            ("blocks", blocks, x_v),
            ("wq", w_q, wq_v),
            ("wkv", w_kv, wkv_v),
            ("prompt", prompt, prm_v),
            ("cache", cache, cache_v),
            ("wo", w_o, wo_v),
            ("wd", w_down, wd_v),
            ("tok", token.at[pl.ds(my_rows, OWN)], tok_v),
        ]
    ):
        loads[name] = pltpu.make_async_copy(src, dst, load_sem.at[i])
    for name in ("gate", "up", "blocks", "wkv", "wq"):
        loads[name].start()

    barrier = pltpu.get_barrier_semaphore()
    partners = [chip(1), chip(2), chip(3), sibling, plane(0, 1), plane(0, 3), plane(1, 0), plane(3, 0), plane(2, 0), plane(0, 2)]
    for who in partners:
        pl.semaphore_signal(barrier, inc=1, device_id=who, device_id_type=MESH)
    pl.semaphore_wait(barrier, len(partners))

    full = (gate_v, up_v)
    sends = ([], [])

    def index(mat, a, b):
        dy, dz = (b, a) if mat == 0 else (a, b)
        return add4(y, dy) * 4 + add4(z, dz)

    def piece(mat, a, b, half):
        start = index(mat, a, b) * SHARD
        if half is None:
            return full[mat].at[pl.ds(pl.multiple_of(start, SHARD), SHARD)]
        return full[mat].at[pl.ds(pl.multiple_of(start + half * (SHARD // 2), SHARD // 2), SHARD // 2)]

    def g_copy(mat, a, b, half, axis, step, send_sem):
        da, db = (step, 0) if axis == 0 else (0, step)
        dy, dz = (db, da) if mat == 0 else (da, db)
        ref = piece(mat, a, b, half)
        return pltpu.make_async_remote_copy(
            src_ref=ref,
            dst_ref=ref,
            send_sem=send_sem,
            recv_sem=g_recv.at[mat, (a - da) % 4, (b - db) % 4, half or 0],
            device_id=plane(dy, dz),
            device_id_type=MESH,
        )

    def g_start(mat, a, b, half, axis, step):
        copy = g_copy(mat, a, b, half, axis, step, g_send.at[mat, len(sends[mat])])
        copy.start()
        sends[mat].append(copy)

    def g_wait(mat, a, b, half=None):
        ref = piece(mat, a, b, half)
        pltpu.make_async_remote_copy(
            src_ref=ref,
            dst_ref=ref,
            send_sem=g_send.at[mat, 0],
            recv_sem=g_recv.at[mat, a % 4, b % 4, half or 0],
            device_id=plane(0, 1),
            device_id_type=MESH,
        ).wait_recv()

    def gather_0():
        for mat, name in ((0, "gate"), (1, "up")):
            loads[name].wait()
            g_start(mat, 0, 0, None, 0, 1)
            g_start(mat, 0, 0, None, 0, -1)

    def turn(mat, axis):
        for step, half in ((1, 0), (-1, 1)):
            at = (-step, 0) if axis == 0 else (0, -step)
            g_wait(mat, *at)
            g_start(mat, *at, half, axis, step)

    def spread(mat, a):
        g_start(mat, a, 0, None, 1, 1)
        g_start(mat, a, 0, None, 1, -1)

    def halves(mat, a, b):
        g_wait(mat, a, b, 0)
        g_wait(mat, a, b, 1)

    def own_onward():
        for mat in (0, 1):
            halves(mat, 2, 0)
        for mat in (0, 1):
            g_start(mat, 0, 0, None, 1, 1)
            g_start(mat, 0, 0, None, 1, -1)

    def forward(mat, a):
        g_wait(mat, a, -1)
        g_start(mat, a, -1, 0, 1, 1)
        g_wait(mat, a, 1)
        g_start(mat, a, 1, 1, 1, -1)

    def tables():
        lane = lax.broadcasted_iota(jnp.int32, (BLOCK, HEAD_DIM), 1)
        row = lax.broadcasted_iota(jnp.int32, (BLOCK, HEAD_DIM), 0)
        for j in range(REQS):
            position = row + (prompt_len[0, 0] + cache_len[0, j])
            angle = position.astype(F32) * frequency[...]
            cos[BLOCK * j : BLOCK * (j + 1), :] = jnp.cos(angle)
            sine = jnp.sin(angle)
            sin[BLOCK * j : BLOCK * (j + 1), :] = jnp.where(lane < HEAD_DIM // 2, -sine, sine)

    def norm_local():
        def step(i, carry):
            rows = pl.ds(pl.multiple_of(i * OWN, OWN), OWN)
            wide = x_v[rows, :].astype(F32)
            scale = lax.rsqrt(jnp.mean(wide * wide, axis=-1, keepdims=True) + EPSILON)
            nrm[rows, :] = (wide * scale * attn_gain[...]).astype(BF16)
            return carry

        lax.fori_loop(0, ROWS // OWN, step, 0)

    def project(ready):
        for k in range(N_AG):
            ready(k)
            cols = slice(k * AG_W, (k + 1) * AG_W)
            lhs = nrm[:, cols]
            q_part = jnp.dot(lhs, wq_v[cols, :], preferred_element_type=F32)
            kv_part = jnp.dot(lhs, wkv_v[cols, :], preferred_element_type=F32)
            if k == 0:
                qkv[:, : HEADS * HEAD_DIM] = q_part
                qkv[:, HEADS * HEAD_DIM :] = kv_part
            else:
                qkv[:, : HEADS * HEAD_DIM] += q_part
                qkv[:, HEADS * HEAD_DIM :] += kv_part

    def attention():
        def rope(values):
            return (values * cos[...] + pltpu.roll(values, HEAD_DIM // 2, 1) * sin[...]).astype(BF16)

        for h in range(HEADS):
            q_s[:, BLOCK * h : BLOCK * (h + 1), :] = rope(
                qkv[:, HEAD_DIM * h : HEAD_DIM * (h + 1)]
            ).reshape(REQS, BLOCK, HEAD_DIM)
        base = HEADS * HEAD_DIM
        k_s[...] = rope(qkv[:, base : base + HEAD_DIM]).reshape(REQS, BLOCK, HEAD_DIM)
        v_s[...] = qkv[:, base + HEAD_DIM :].astype(BF16).reshape(REQS, BLOCK, HEAD_DIM)
        scale = math.log2(math.e) / math.sqrt(HEAD_DIM)
        contract = (((1,), (1,)), ((), ()))

        def step(j, carry):
            q = q_s[j]

            def scores(keys):
                return lax.dot_general(q, keys, contract, preferred_element_type=F32) * scale

            s_c = scores(cache_v[j, :, :HEAD_DIM])
            s_p = scores(prm_v[:, :HEAD_DIM])
            s_b = scores(k_s[j])
            at_c = lax.broadcasted_iota(jnp.int32, s_c.shape, 1)
            at_p = lax.broadcasted_iota(jnp.int32, s_p.shape, 1)
            s_c = jnp.where(at_c < cache_len[0, j], s_c, -1e30)
            s_p = jnp.where(at_p < prompt_len[0, 0], s_p, -1e30)
            top = jnp.maximum(
                jnp.maximum(jnp.max(s_c, -1, keepdims=True), jnp.max(s_p, -1, keepdims=True)),
                jnp.max(s_b, -1, keepdims=True),
            )
            e_c = jnp.exp2(s_c - top)
            e_p = jnp.exp2(s_p - top)
            e_b = jnp.exp2(s_b - top)
            total = (
                jnp.sum(e_c, -1, keepdims=True)
                + jnp.sum(e_p, -1, keepdims=True)
                + jnp.sum(e_b, -1, keepdims=True)
            )
            mixed = jnp.dot(e_c.astype(BF16), cache_v[j, :, HEAD_DIM:], preferred_element_type=F32)
            mixed += jnp.dot(e_p.astype(BF16), prm_v[:, HEAD_DIM:], preferred_element_type=F32)
            mixed += jnp.dot(e_b.astype(BF16), v_s[j], preferred_element_type=F32)
            mixed = (mixed / total).astype(BF16)
            for h in range(HEADS):
                att[j, :, HEAD_DIM * h : HEAD_DIM * (h + 1)] = mixed[BLOCK * h : BLOCK * (h + 1)]
            return carry

        lax.fori_loop(0, REQS, step, 0, unroll=4)

    pending = []

    def reduce_scatter(lhs, weight):
        def chips(n):
            sib_copies[n].wait_recv()
            total = part[n, pl.ds(my_half, 64), :] + sib_in[n].astype(F32)
            part[n, pl.ds(my_half, 64), :] = total
            x_out[n] = total.astype(BF16).reshape(4, OWN, RS_W)
            for d in (2, 1, 3):
                copy = pltpu.make_async_remote_copy(
                    src_ref=x_out.at[n, add4(x, d)],
                    dst_ref=x_in.at[n, d],
                    send_sem=x_ss.at[n, d],
                    recv_sem=x_rs.at[n, d],
                    device_id=chip(d),
                    device_id_type=MESH,
                )
                copy.start()
                x_copies.append(copy)

        sib_copies, x_copies = [], []
        for n in range(N_RS):
            part[n] = jnp.dot(lhs, weight[:, n * RS_W : (n + 1) * RS_W], preferred_element_type=F32)
            sib_out[n] = part[n, pl.ds(other_half, 64), :].astype(BF16)
            copy = pltpu.make_async_remote_copy(
                src_ref=sib_out.at[n],
                dst_ref=sib_in.at[n],
                send_sem=sib_ss.at[n],
                recv_sem=sib_rs.at[n],
                device_id=sibling,
                device_id_type=MESH,
            )
            copy.start()
            sib_copies.append(copy)
            if n > 0:
                chips(n - 1)
        chips(N_RS - 1)

        def own(n):
            total = part[n, pl.ds(my_rows, OWN), :]
            for i, d in enumerate((2, 1, 3)):
                x_copies[3 * n + i].wait_recv()
                total = total + x_in[n, d].astype(F32)
            return total

        def finish():
            for copy in sib_copies + x_copies:
                copy.wait_send()

        return own, finish

    def normalize(square_sum, gain):
        scale = lax.rsqrt(square_sum / D + EPSILON)
        for n in range(N_RS):
            cols = slice(n * RS_W, (n + 1) * RS_W)
            nrm[pl.ds(my_rows, OWN), cols] = (res[:, cols] * scale * gain[:, cols]).astype(BF16)

    def share_rows():
        ag = {}

        def copy_rows(k, row, send, recv, who):
            ref = nrm.at[pl.ds(pl.multiple_of(row, OWN), OWN), pl.ds(k * AG_W, AG_W)]
            return pltpu.make_async_remote_copy(
                src_ref=ref, dst_ref=ref, send_sem=send, recv_sem=recv, device_id=who, device_id_type=MESH
            )

        for k in range(N_AG):
            for d in (2, 1, 3):
                ag[k, d] = copy_rows(k, my_rows, agx_s.at[k, d], agx_r.at[k, d], chip(d))
                ag[k, d].start()
            ag[k, 4] = copy_rows(k, my_rows, ags_s.at[k, 0], ags_r.at[k, 0], sibling)
            ag[k, 4].start()

        def ready(k):
            for d in (1, 3, 2):
                row = 64 * c + OWN * add4(x, -d)
                copy_rows(k, row, agx_s.at[k, d], agx_r.at[k, d], sibling).wait_recv()
                ag[k, 4 + d] = copy_rows(k, row, ags_s.at[k, d], ags_r.at[k, d], sibling)
                ag[k, 4 + d].start()
            for d in (0, 1, 3, 2):
                row = 64 * (1 - c) + OWN * add4(x, -d)
                copy_rows(k, row, ags_s.at[k, d], ags_r.at[k, d], sibling).wait_recv()

        def finish():
            for copy in ag.values():
                copy.wait_send()

        return ready, finish

    def after_attention(own, gain):
        square_sum = jnp.zeros((OWN, 1), F32)
        for n in range(N_RS):
            cols = slice(n * RS_W, (n + 1) * RS_W)
            total = (res[:, cols] + own(n)).astype(BF16).astype(F32)
            res[:, cols] = total
            square_sum += jnp.sum(total * total, axis=-1, keepdims=True)
        normalize(square_sum, gain)

    def between_passes(own):
        lane = lax.broadcasted_iota(jnp.int32, (OWN, ROWS), 1)
        row = lax.broadcasted_iota(jnp.int32, (OWN, ROWS), 0) + my_rows
        mine = jnp.where(lane == row, accepted[...].astype(F32), 0.0)
        take = jnp.sum(mine, axis=-1, keepdims=True) == 1.0
        square_sum = jnp.zeros((OWN, 1), F32)
        for n in range(N_RS):
            cols = slice(n * RS_W, (n + 1) * RS_W)
            first = (res[:, cols] + own(n)).astype(BF16).astype(F32)
            total = jnp.where(take, tok_v[:, cols].astype(F32), first)
            res[:, cols] = total
            square_sum += jnp.sum(total * total, axis=-1, keepdims=True)
        normalize(square_sum, attn_gain)

    def activate():
        gate = g_acc[...]
        hid[...] = (gate / (1.0 + jnp.exp(-gate)) * u_acc[...]).astype(BF16)

    def along(mat, d):
        return plane(d, 0) if mat == 0 else plane(0, d)

    def slice_rows(meanwhile):
        made = {}

        def go(key, src, dst, send, recv, who):
            made[key] = pltpu.make_async_remote_copy(
                src_ref=src, dst_ref=dst, send_sem=send, recv_sem=recv, device_id=who, device_id_type=MESH
            )
            made[key].start()

        def rows_of(mat, k, core, d):
            row = 64 * core + OWN * add4(x, d)
            return rows_k.at[mat, k, pl.ds(pl.multiple_of(row, OWN), OWN)]

        def chunk(mat, d):
            if mat == 0:
                at = pl.ds(pl.multiple_of(add4(y, d) * SLICE, SLICE), SLICE)
                return nrm.at[pl.ds(my_rows, OWN), at]
            return strided.at[add4(z, d)]

        def over_x(mat, k):
            ref = rows_of(mat, k, c, 0)
            for d in (2, 1, 3):
                go(("x", mat, k, d), ref, ref, kx_s.at[mat, k, d], kx_r.at[mat, k, d], chip(d))
            go(("s", mat, k, 0), ref, ref, ks_s.at[mat, k, 0], ks_r.at[mat, k, 0], sibling)

        for i in range(4):
            for j in range(4):
                start = SLICE * j + SHARD * i
                strided[i, :, SHARD * j : SHARD * (j + 1)] = nrm[
                    pl.ds(my_rows, OWN), start : start + SHARD
                ]
        for d in (2, 1, 3):
            for mat in (0, 1):
                k = (-d) % 4
                go(
                    ("p", mat, k), chunk(mat, d), rows_of(mat, k, c, 0),
                    ky_s.at[mat, k], ky_r.at[mat, k], along(mat, d),
                )
        for mat in (0, 1):
            rows_k[mat, 0, pl.ds(my_rows, OWN), :] = chunk(mat, 0)[...]
        for mat in (0, 1):
            over_x(mat, 0)
        for k in (2, 1, 3):
            for mat in (0, 1):
                made["p", mat, k].wait_recv()
                over_x(mat, k)
        meanwhile()

        def ready(mat, k):
            for d in (1, 3, 2):
                made["x", mat, k, d].wait_recv()
                ref = rows_of(mat, k, c, -d)
                go(("s", mat, k, d), ref, ref, ks_s.at[mat, k, d], ks_r.at[mat, k, d], sibling)
            for d in (0, 1, 3, 2):
                made["s", mat, k, d].wait_recv()

        def finish():
            for copy in made.values():
                copy.wait_send()

        return ready, finish

    def slice_gate_up(ready):
        made = []
        accs = (g_acc, u_acc)
        half = ROWS // 2

        def product(mat, k):
            if mat == 0:
                at = pl.ds(pl.multiple_of(y * SLICE, SLICE), SLICE)
                return jnp.dot(rows_k[0, k], gate_v[at, :], preferred_element_type=F32)
            total = jnp.zeros((ROWS, HIDDEN), F32)
            for j in range(4):
                at = pl.ds(pl.multiple_of((4 * j + z) * SHARD, SHARD), SHARD)
                lhs = rows_k[1, k, :, SHARD * j : SHARD * (j + 1)]
                total += jnp.dot(lhs, up_v[at, :], preferred_element_type=F32)
            return total

        def go(src, dst, send, recv, who):
            copy = pltpu.make_async_remote_copy(
                src_ref=src, dst_ref=dst, send_sem=send, recv_sem=recv, device_id=who, device_id_type=MESH
            )
            copy.start()
            made.append(copy)
            return copy

        far = {}
        for mat in (0, 1):
            ready(mat, 2)
            value = product(mat, 2).astype(BF16)
            for i in (0, 1):
                far_out[mat, i] = value[half * i : half * (i + 1)]
                far[mat, i] = go(
                    far_out.at[mat, i], far_in.at[mat, i], far_s.at[mat, i], far_r.at[mat, i],
                    along(mat, 1 - 2 * i),
                )
        near = []

        def send_near(i, mat, part_i):
            near.append(
                go(
                    near_out.at[i, mat, part_i], near_in.at[i, mat, part_i],
                    near_s.at[i, mat, part_i], near_r.at[i, mat, part_i], along(mat, 1 - 2 * i),
                )
            )

        for i in (0, 1):
            for mat in (0, 1):
                ready(mat, 1 + 2 * i)
                value = product(mat, 1 + 2 * i)
                near_keep[i, mat] = value[half * i : half * (i + 1)]
                near_out[i, mat, 1 - i] = value[half * (1 - i) : half * (2 - i)].astype(BF16)
                send_near(i, mat, 1 - i)
        for i in (0, 1):
            for mat in (0, 1):
                far[mat, i].wait_recv()
                near_out[i, mat, i] = (near_keep[i, mat] + far_in[mat, i].astype(F32)).astype(BF16)
                send_near(i, mat, i)
        for mat in (0, 1):
            ready(mat, 0)
            accs[mat][...] = product(mat, 0)

        def collect():
            for copy in near:
                copy.wait_recv()
            for mat in (0, 1):
                for i in (0, 1):
                    rows = slice(half * i, half * (i + 1))
                    accs[mat][rows, :] += near_in[0, mat, i].astype(F32) + near_in[1, mat, i].astype(F32)

        def finish():
            for copy in made:
                copy.wait_send()

        return collect, finish

    def attended():
        return att[...].reshape(ROWS, HEADS * HEAD_DIM)

    gather_0()
    tables()
    loads["blocks"].wait()
    norm_local()
    res[...] = x_v[pl.ds(my_rows, OWN), :].astype(F32)
    loads["wq"].wait()
    loads["wkv"].wait()
    for name in ("prompt", "cache", "wo", "wd", "tok"):
        loads[name].start()
    project(lambda k: None)
    loads["prompt"].wait()
    loads["cache"].wait()
    attention()
    loads["wo"].wait()
    own, rs_done = reduce_scatter(attended(), wo_v)
    for mat in (0, 1):
        turn(mat, 0)
    after_attention(own, mlp_gain)
    rs_done()
    ready, rows_done = slice_rows(own_onward)
    collect, sums_done = slice_gate_up(ready)
    collect()
    for mat in (0, 1):
        turn(mat, 1)
        spread(mat, -1)
        spread(mat, 1)
    rows_done()
    sums_done()
    activate()
    loads["wd"].wait()
    loads["tok"].wait()
    own, rs_done = reduce_scatter(hid[...], wd_v)
    between_passes(own)
    rs_done()

    ready, ag_done = share_rows()
    project(ready)
    ag_done()
    for mat in (0, 1):
        forward(mat, -1)
        spread(mat, 2)
    attention()
    for mat in (0, 1):
        forward(mat, 1)
    own, rs_done = reduce_scatter(attended(), wo_v)
    after_attention(own, mlp_gain)
    rs_done()
    ready, ag_done = share_rows()
    for mat in (0, 1):
        forward(mat, 2)
    for a in (0, -1, 1, 2):
        halves(0, a, 2)
        halves(1, a, 2)
    for k in range(N_AG):
        ready(k)
        for part_k in range(2):
            start = k * AG_W + part_k * (AG_W // 2)
            at = slice(start, start + AG_W // 2)
            for acc, weight in ((g_acc, gate_v), (u_acc, up_v)):
                product = jnp.dot(nrm[:, at], weight[at, :], preferred_element_type=F32)
                if start == 0:
                    acc[...] = product
                else:
                    acc[...] += product
    ag_done()
    for copy in sends[0] + sends[1]:
        copy.wait_send()
    activate()
    own, rs_done = reduce_scatter(hid[...], wd_v)
    for n in range(N_RS):
        cols = slice(n * RS_W, (n + 1) * RS_W)
        nrm[pl.ds(my_rows, OWN), cols] = (res[:, cols] + own(n)).astype(BF16)
    rs_done()
    ready, ag_done = share_rows()
    for k in range(N_AG):
        ready(k)
    ag_done()
    copy = pltpu.make_async_copy(nrm, out, load_sem.at[0])
    copy.start()
    copy.wait()


def body(
    blocks, token_embed, accepted, prompt_len, cache_len, prompt_kv, cache_kv, attn_gain,
    w_q, w_kv, w_o, mlp_gain, w_gate, w_up, w_down,
):
    half = np.arange(HEAD_DIM // 2, dtype=np.float32)
    frequency = np.float32(THETA) ** (np.float32(-2.0) * half / np.float32(HEAD_DIM))
    frequency = jnp.asarray(np.concatenate([frequency, frequency])[None, :], dtype=F32)

    vmem = pl.BlockSpec(memory_space=pltpu.VMEM)
    anywhere = pl.BlockSpec(memory_space=pl.ANY)
    dma = pltpu.SemaphoreType.DMA
    return pl.pallas_call(
        kernel,
        out_shape=jax.ShapeDtypeStruct((ROWS, D), BF16),
        in_specs=[pl.BlockSpec(memory_space=pltpu.SMEM)] * 2 + [vmem] * 4 + [anywhere] * 10,
        out_specs=anywhere,
        scratch_shapes=[
            pltpu.VMEM((ROWS, D), BF16),
            pltpu.VMEM((OWN, D), BF16),
            pltpu.VMEM((PMAX, 2 * HEAD_DIM), BF16),
            pltpu.VMEM((REQS, CACHE, 2 * HEAD_DIM), BF16),
            pltpu.VMEM((D, HEADS * HEAD_DIM), BF16),
            pltpu.VMEM((D, 2 * HEAD_DIM), BF16),
            pltpu.VMEM((HEADS * HEAD_DIM, D), BF16),
            pltpu.VMEM((D, HIDDEN), BF16),
            pltpu.VMEM((D, HIDDEN), BF16),
            pltpu.VMEM((HIDDEN, D), BF16),
            pltpu.VMEM((ROWS, D), BF16),
            pltpu.VMEM((ROWS, (HEADS + 2) * HEAD_DIM), F32),
            pltpu.VMEM((REQS, HEADS * BLOCK, HEAD_DIM), BF16),
            pltpu.VMEM((REQS, BLOCK, HEAD_DIM), BF16),
            pltpu.VMEM((REQS, BLOCK, HEAD_DIM), BF16),
            pltpu.VMEM((REQS, BLOCK, HEADS * HEAD_DIM), BF16),
            pltpu.VMEM((ROWS, HIDDEN), F32),
            pltpu.VMEM((ROWS, HIDDEN), F32),
            pltpu.VMEM((ROWS, HIDDEN), BF16),
            pltpu.VMEM((N_RS, ROWS, RS_W), F32),
            pltpu.VMEM((N_RS, 64, RS_W), BF16),
            pltpu.VMEM((N_RS, 64, RS_W), BF16),
            pltpu.VMEM((N_RS, 4, OWN, RS_W), BF16),
            pltpu.VMEM((N_RS, 4, OWN, RS_W), BF16),
            pltpu.VMEM((OWN, D), F32),
            pltpu.VMEM((ROWS, HEAD_DIM), F32),
            pltpu.VMEM((ROWS, HEAD_DIM), F32),
            pltpu.VMEM((4, OWN, SLICE), BF16),
            pltpu.VMEM((2, 4, ROWS, SLICE), BF16),
            pltpu.VMEM((2, 2, ROWS // 2, HIDDEN), BF16),
            pltpu.VMEM((2, 2, ROWS // 2, HIDDEN), BF16),
            pltpu.VMEM((2, 2, ROWS // 2, HIDDEN), F32),
            pltpu.VMEM((2, 2, 2, ROWS // 2, HIDDEN), BF16),
            pltpu.VMEM((2, 2, 2, ROWS // 2, HIDDEN), BF16),
            dma((10,)),
            dma((2, 20)),
            dma((2, 4, 4, 2)),
            dma((N_RS,)),
            dma((N_RS,)),
            dma((N_RS, 4)),
            dma((N_RS, 4)),
            dma((N_AG, 4)),
            dma((N_AG, 4)),
            dma((N_AG, 4)),
            dma((N_AG, 4)),
            dma((2, 4)),
            dma((2, 4)),
            dma((2, 4, 4)),
            dma((2, 4, 4)),
            dma((2, 4, 4)),
            dma((2, 4, 4)),
            dma((2, 2)),
            dma((2, 2)),
            dma((2, 2, 2)),
            dma((2, 2, 2)),
        ],
        compiler_params=pltpu.CompilerParams(
            collective_id=0, has_side_effects=True, vmem_limit_bytes=60 * 2**20
        ),
        name="two_passes",
    )(
        prompt_len[None, :], cache_len, accepted[None, :], frequency, attn_gain[None, :], mlp_gain[None, :],
        blocks, token_embed, prompt_kv[0], cache_kv[0], w_q, w_kv, w_o, w_gate, w_up, w_down,
    )


def solution(mesh):
    return jax.shard_map(
        body,
        mesh=mesh,
        in_specs=(
            P("req", None),
            P("req", None),
            P("req"),
            P("req"),
            P("req", None),
            P("req", None, "mlp"),
            P("req", None, None, "mlp"),
            P(),
            P(None, "mlp"),
            P(None, "mlp"),
            P("mlp", None),
            P(),
            P("req", "mlp"),
            P("req", "mlp"),
            P("mlp", None),
        ),
        out_specs=P("req", None),
        check_vma=False,
    )
```

```python
import math

import jax
import jax.numpy as jnp
from jax import lax
from jax.experimental import pallas as pl
from jax.experimental.pallas import tpu as pltpu
from jax.sharding import PartitionSpec as P
import numpy as np

D = 4096
HEAD_DIM = 128
HEADS = 4
REQS = 8
BLOCK = 16
ROWS = REQS * BLOCK
CACHE = 1024
PMAX = 512
HIDDEN = 896
SHARD = 256
SLICE = 1024
OWN = 16
EPSILON = 1e-05
THETA = 500000.0
MESH = pl.DeviceIdType.MESH
N_RS = 4
RS_W = D // N_RS
N_AG = 2
AG_W = D // N_AG
F32 = jnp.float32
BF16 = jnp.bfloat16


def kernel(
    prompt_len, cache_len, accepted, frequency, attn_gain, mlp_gain,
    blocks, token, prompt, cache, w_q, w_kv, w_o, w_gate, w_up, w_down,
    out,
    x_v, tok_v, prm_v, cache_v, wq_v, wkv_v, wo_v, gate_v, up_v, wd_v,
    nrm, qkv, q_s, k_s, v_s, att, g_acc, u_acc, hid,
    part, sib_out, sib_in, x_out, x_in, res, cos, sin,
    strided, rows_k, far_out, far_in, near_keep, near_out, near_in,
    load_sem, g_send, g_recv, sib_ss, sib_rs, x_ss, x_rs, agx_s, agx_r, ags_s, ags_r,
    ky_s, ky_r, kx_s, kx_r, ks_s, ks_r, far_s, far_r, near_s, near_r,
):
    r = lax.axis_index("req")
    m = lax.axis_index("mlp")
    y, z = lax.div(r, 4), lax.rem(r, 4)
    x, c = lax.div(m, 2), lax.rem(m, 2)

    def add4(v, d):
        return lax.rem(v + (d % 4), 4)

    def chip(d):
        return (r, add4(x, d) * 2 + c)

    sibling = (r, x * 2 + 1 - c)

    def plane(dy, dz):
        return (add4(y, dy) * 4 + add4(z, dz), m)

    my_half = pl.multiple_of(64 * c, 64)
    other_half = pl.multiple_of(64 * (1 - c), 64)
    my_rows = pl.multiple_of(64 * c + OWN * x, OWN)

    own_shard = pl.ds(pl.multiple_of(r * SHARD, SHARD), SHARD)
    loads = {}
    for i, (name, src, dst) in enumerate(
        [
            ("gate", w_gate, gate_v.at[own_shard]),
            ("up", w_up, up_v.at[own_shard]),
            ("blocks", blocks, x_v),
            ("wq", w_q, wq_v),
            ("wkv", w_kv, wkv_v),
            ("prompt", prompt, prm_v),
            ("cache", cache, cache_v),
            ("wo", w_o, wo_v),
            ("wd", w_down, wd_v),
            ("tok", token.at[pl.ds(my_rows, OWN)], tok_v),
        ]
    ):
        loads[name] = pltpu.make_async_copy(src, dst, load_sem.at[i])
    for name in ("gate", "up", "blocks", "wkv", "wq"):
        loads[name].start()

    barrier = pltpu.get_barrier_semaphore()
    partners = [chip(1), chip(2), chip(3), sibling, plane(0, 1), plane(0, 3), plane(1, 0), plane(3, 0), plane(2, 0), plane(0, 2)]
    for who in partners:
        pl.semaphore_signal(barrier, inc=1, device_id=who, device_id_type=MESH)
    pl.semaphore_wait(barrier, len(partners))

    full = (gate_v, up_v)
    sends = ([], [])

    def index(mat, a, b):
        dy, dz = (b, a) if mat == 0 else (a, b)
        return add4(y, dy) * 4 + add4(z, dz)

    def piece(mat, a, b, half):
        start = index(mat, a, b) * SHARD
        if half is None:
            return full[mat].at[pl.ds(pl.multiple_of(start, SHARD), SHARD)]
        return full[mat].at[pl.ds(pl.multiple_of(start + half * (SHARD // 2), SHARD // 2), SHARD // 2)]

    def g_copy(mat, a, b, half, axis, step, send_sem):
        da, db = (step, 0) if axis == 0 else (0, step)
        dy, dz = (db, da) if mat == 0 else (da, db)
        ref = piece(mat, a, b, half)
        return pltpu.make_async_remote_copy(
            src_ref=ref,
            dst_ref=ref,
            send_sem=send_sem,
            recv_sem=g_recv.at[mat, (a - da) % 4, (b - db) % 4, half or 0],
            device_id=plane(dy, dz),
            device_id_type=MESH,
        )

    def g_start(mat, a, b, half, axis, step):
        copy = g_copy(mat, a, b, half, axis, step, g_send.at[mat, len(sends[mat])])
        copy.start()
        sends[mat].append(copy)

    def g_wait(mat, a, b, half=None):
        ref = piece(mat, a, b, half)
        pltpu.make_async_remote_copy(
            src_ref=ref,
            dst_ref=ref,
            send_sem=g_send.at[mat, 0],
            recv_sem=g_recv.at[mat, a % 4, b % 4, half or 0],
            device_id=plane(0, 1),
            device_id_type=MESH,
        ).wait_recv()

    def gather_0():
        for mat, name in ((0, "gate"), (1, "up")):
            loads[name].wait()
            g_start(mat, 0, 0, None, 0, 1)
            g_start(mat, 0, 0, None, 0, -1)

    def turn(mat, axis):
        for step, half in ((1, 0), (-1, 1)):
            at = (-step, 0) if axis == 0 else (0, -step)
            g_wait(mat, *at)
            g_start(mat, *at, half, axis, step)

    def spread(mat, a):
        g_start(mat, a, 0, None, 1, 1)
        g_start(mat, a, 0, None, 1, -1)

    def halves(mat, a, b):
        g_wait(mat, a, b, 0)
        g_wait(mat, a, b, 1)

    def own_onward():
        for mat in (0, 1):
            halves(mat, 2, 0)
        for mat in (0, 1):
            g_start(mat, 0, 0, None, 1, 1)
            g_start(mat, 0, 0, None, 1, -1)

    def forward(mat, a):
        g_wait(mat, a, -1)
        g_start(mat, a, -1, 0, 1, 1)
        g_wait(mat, a, 1)
        g_start(mat, a, 1, 1, 1, -1)

    def tables():
        lane = lax.broadcasted_iota(jnp.int32, (BLOCK, HEAD_DIM), 1)
        row = lax.broadcasted_iota(jnp.int32, (BLOCK, HEAD_DIM), 0)
        for j in range(REQS):
            position = row + (prompt_len[0, 0] + cache_len[0, j])
            angle = position.astype(F32) * frequency[...]
            cos[BLOCK * j : BLOCK * (j + 1), :] = jnp.cos(angle)
            sine = jnp.sin(angle)
            sin[BLOCK * j : BLOCK * (j + 1), :] = jnp.where(lane < HEAD_DIM // 2, -sine, sine)

    def norm_local():
        def step(i, carry):
            rows = pl.ds(pl.multiple_of(i * OWN, OWN), OWN)
            wide = x_v[rows, :].astype(F32)
            scale = lax.rsqrt(jnp.mean(wide * wide, axis=-1, keepdims=True) + EPSILON)
            nrm[rows, :] = (wide * scale * attn_gain[...]).astype(BF16)
            return carry

        lax.fori_loop(0, ROWS // OWN, step, 0)

    def project(ready):
        for k in range(N_AG):
            ready(k)
            cols = slice(k * AG_W, (k + 1) * AG_W)
            lhs = nrm[:, cols]
            q_part = jnp.dot(lhs, wq_v[cols, :], preferred_element_type=F32)
            kv_part = jnp.dot(lhs, wkv_v[cols, :], preferred_element_type=F32)
            if k == 0:
                qkv[:, : HEADS * HEAD_DIM] = q_part
                qkv[:, HEADS * HEAD_DIM :] = kv_part
            else:
                qkv[:, : HEADS * HEAD_DIM] += q_part
                qkv[:, HEADS * HEAD_DIM :] += kv_part

    def attention():
        def rope(values):
            return (values * cos[...] + pltpu.roll(values, HEAD_DIM // 2, 1) * sin[...]).astype(BF16)

        for h in range(HEADS):
            q_s[:, BLOCK * h : BLOCK * (h + 1), :] = rope(
                qkv[:, HEAD_DIM * h : HEAD_DIM * (h + 1)]
            ).reshape(REQS, BLOCK, HEAD_DIM)
        base = HEADS * HEAD_DIM
        k_s[...] = rope(qkv[:, base : base + HEAD_DIM]).reshape(REQS, BLOCK, HEAD_DIM)
        v_s[...] = qkv[:, base + HEAD_DIM :].astype(BF16).reshape(REQS, BLOCK, HEAD_DIM)
        scale = math.log2(math.e) / math.sqrt(HEAD_DIM)
        contract = (((1,), (1,)), ((), ()))

        def step(j, carry):
            q = q_s[j]

            def scores(keys):
                return lax.dot_general(q, keys, contract, preferred_element_type=F32) * scale

            s_c = scores(cache_v[j, :, :HEAD_DIM])
            s_p = scores(prm_v[:, :HEAD_DIM])
            s_b = scores(k_s[j])
            at_c = lax.broadcasted_iota(jnp.int32, s_c.shape, 1)
            at_p = lax.broadcasted_iota(jnp.int32, s_p.shape, 1)
            s_c = jnp.where(at_c < cache_len[0, j], s_c, -1e30)
            s_p = jnp.where(at_p < prompt_len[0, 0], s_p, -1e30)
            top = jnp.maximum(
                jnp.maximum(jnp.max(s_c, -1, keepdims=True), jnp.max(s_p, -1, keepdims=True)),
                jnp.max(s_b, -1, keepdims=True),
            )
            e_c = jnp.exp2(s_c - top)
            e_p = jnp.exp2(s_p - top)
            e_b = jnp.exp2(s_b - top)
            total = (
                jnp.sum(e_c, -1, keepdims=True)
                + jnp.sum(e_p, -1, keepdims=True)
                + jnp.sum(e_b, -1, keepdims=True)
            )
            mixed = jnp.dot(e_c.astype(BF16), cache_v[j, :, HEAD_DIM:], preferred_element_type=F32)
            mixed += jnp.dot(e_p.astype(BF16), prm_v[:, HEAD_DIM:], preferred_element_type=F32)
            mixed += jnp.dot(e_b.astype(BF16), v_s[j], preferred_element_type=F32)
            mixed = (mixed / total).astype(BF16)
            for h in range(HEADS):
                att[j, :, HEAD_DIM * h : HEAD_DIM * (h + 1)] = mixed[BLOCK * h : BLOCK * (h + 1)]
            return carry

        lax.fori_loop(0, REQS, step, 0, unroll=4)

    pending = []

    def reduce_scatter(lhs, weight):
        def chips(n):
            sib_copies[n].wait_recv()
            total = part[n, pl.ds(my_half, 64), :] + sib_in[n].astype(F32)
            part[n, pl.ds(my_half, 64), :] = total
            x_out[n] = total.astype(BF16).reshape(4, OWN, RS_W)
            for d in (2, 1, 3):
                copy = pltpu.make_async_remote_copy(
                    src_ref=x_out.at[n, add4(x, d)],
                    dst_ref=x_in.at[n, d],
                    send_sem=x_ss.at[n, d],
                    recv_sem=x_rs.at[n, d],
                    device_id=chip(d),
                    device_id_type=MESH,
                )
                copy.start()
                x_copies.append(copy)

        sib_copies, x_copies = [], []
        for n in range(N_RS):
            part[n] = jnp.dot(lhs, weight[:, n * RS_W : (n + 1) * RS_W], preferred_element_type=F32)
            sib_out[n] = part[n, pl.ds(other_half, 64), :].astype(BF16)
            copy = pltpu.make_async_remote_copy(
                src_ref=sib_out.at[n],
                dst_ref=sib_in.at[n],
                send_sem=sib_ss.at[n],
                recv_sem=sib_rs.at[n],
                device_id=sibling,
                device_id_type=MESH,
            )
            copy.start()
            sib_copies.append(copy)
            if n > 0:
                chips(n - 1)
        chips(N_RS - 1)

        def own(n):
            total = part[n, pl.ds(my_rows, OWN), :]
            for i, d in enumerate((2, 1, 3)):
                x_copies[3 * n + i].wait_recv()
                total = total + x_in[n, d].astype(F32)
            return total

        def finish():
            for copy in sib_copies + x_copies:
                copy.wait_send()

        return own, finish

    def normalize(square_sum, gain):
        scale = lax.rsqrt(square_sum / D + EPSILON)
        for n in range(N_RS):
            cols = slice(n * RS_W, (n + 1) * RS_W)
            nrm[pl.ds(my_rows, OWN), cols] = (res[:, cols] * scale * gain[:, cols]).astype(BF16)

    def share_rows():
        ag = {}

        def copy_rows(k, row, send, recv, who):
            ref = nrm.at[pl.ds(pl.multiple_of(row, OWN), OWN), pl.ds(k * AG_W, AG_W)]
            return pltpu.make_async_remote_copy(
                src_ref=ref, dst_ref=ref, send_sem=send, recv_sem=recv, device_id=who, device_id_type=MESH
            )

        for k in range(N_AG):
            for d in (2, 1, 3):
                ag[k, d] = copy_rows(k, my_rows, agx_s.at[k, d], agx_r.at[k, d], chip(d))
                ag[k, d].start()
            ag[k, 4] = copy_rows(k, my_rows, ags_s.at[k, 0], ags_r.at[k, 0], sibling)
            ag[k, 4].start()

        def ready(k):
            for d in (1, 3, 2):
                row = 64 * c + OWN * add4(x, -d)
                copy_rows(k, row, agx_s.at[k, d], agx_r.at[k, d], sibling).wait_recv()
                ag[k, 4 + d] = copy_rows(k, row, ags_s.at[k, d], ags_r.at[k, d], sibling)
                ag[k, 4 + d].start()
            for d in (0, 1, 3, 2):
                row = 64 * (1 - c) + OWN * add4(x, -d)
                copy_rows(k, row, ags_s.at[k, d], ags_r.at[k, d], sibling).wait_recv()

        def finish():
            for copy in ag.values():
                copy.wait_send()

        return ready, finish

    def after_attention(own, gain):
        square_sum = jnp.zeros((OWN, 1), F32)
        for n in range(N_RS):
            cols = slice(n * RS_W, (n + 1) * RS_W)
            total = (res[:, cols] + own(n)).astype(BF16).astype(F32)
            res[:, cols] = total
            square_sum += jnp.sum(total * total, axis=-1, keepdims=True)
        normalize(square_sum, gain)

    def between_passes(own):
        lane = lax.broadcasted_iota(jnp.int32, (OWN, ROWS), 1)
        row = lax.broadcasted_iota(jnp.int32, (OWN, ROWS), 0) + my_rows
        mine = jnp.where(lane == row, accepted[...].astype(F32), 0.0)
        take = jnp.sum(mine, axis=-1, keepdims=True) == 1.0
        square_sum = jnp.zeros((OWN, 1), F32)
        for n in range(N_RS):
            cols = slice(n * RS_W, (n + 1) * RS_W)
            first = (res[:, cols] + own(n)).astype(BF16).astype(F32)
            total = jnp.where(take, tok_v[:, cols].astype(F32), first)
            res[:, cols] = total
            square_sum += jnp.sum(total * total, axis=-1, keepdims=True)
        normalize(square_sum, attn_gain)

    def activate():
        gate = g_acc[...]
        hid[...] = (gate / (1.0 + jnp.exp(-gate)) * u_acc[...]).astype(BF16)

    def along(mat, d):
        return plane(d, 0) if mat == 0 else plane(0, d)

    def slice_rows(meanwhile):
        made = {}

        def go(key, src, dst, send, recv, who):
            made[key] = pltpu.make_async_remote_copy(
                src_ref=src, dst_ref=dst, send_sem=send, recv_sem=recv, device_id=who, device_id_type=MESH
            )
            made[key].start()

        def rows_of(mat, k, core, d):
            row = 64 * core + OWN * add4(x, d)
            return rows_k.at[mat, k, pl.ds(pl.multiple_of(row, OWN), OWN)]

        def chunk(mat, d):
            if mat == 0:
                at = pl.ds(pl.multiple_of(add4(y, d) * SLICE, SLICE), SLICE)
                return nrm.at[pl.ds(my_rows, OWN), at]
            return strided.at[add4(z, d)]

        def over_x(mat, k):
            ref = rows_of(mat, k, c, 0)
            for d in (2, 1, 3):
                go(("x", mat, k, d), ref, ref, kx_s.at[mat, k, d], kx_r.at[mat, k, d], chip(d))
            go(("s", mat, k, 0), ref, ref, ks_s.at[mat, k, 0], ks_r.at[mat, k, 0], sibling)

        for i in range(4):
            for j in range(4):
                start = SLICE * j + SHARD * i
                strided[i, :, SHARD * j : SHARD * (j + 1)] = nrm[
                    pl.ds(my_rows, OWN), start : start + SHARD
                ]
        for d in (2, 1, 3):
            for mat in (0, 1):
                k = (-d) % 4
                go(
                    ("p", mat, k), chunk(mat, d), rows_of(mat, k, c, 0),
                    ky_s.at[mat, k], ky_r.at[mat, k], along(mat, d),
                )
        for mat in (0, 1):
            rows_k[mat, 0, pl.ds(my_rows, OWN), :] = chunk(mat, 0)[...]
        for mat in (0, 1):
            over_x(mat, 0)
        for k in (2, 1, 3):
            for mat in (0, 1):
                made["p", mat, k].wait_recv()
                over_x(mat, k)
        meanwhile()

        def ready(mat, k):
            for d in (1, 3, 2):
                made["x", mat, k, d].wait_recv()
                ref = rows_of(mat, k, c, -d)
                go(("s", mat, k, d), ref, ref, ks_s.at[mat, k, d], ks_r.at[mat, k, d], sibling)
            for d in (0, 1, 3, 2):
                made["s", mat, k, d].wait_recv()

        def finish():
            for copy in made.values():
                copy.wait_send()

        return ready, finish

    def slice_gate_up(ready):
        made = []
        accs = (g_acc, u_acc)
        half = ROWS // 2

        def product(mat, k):
            if mat == 0:
                at = pl.ds(pl.multiple_of(y * SLICE, SLICE), SLICE)
                return jnp.dot(rows_k[0, k], gate_v[at, :], preferred_element_type=F32)
            total = jnp.zeros((ROWS, HIDDEN), F32)
            for j in range(4):
                at = pl.ds(pl.multiple_of((4 * j + z) * SHARD, SHARD), SHARD)
                lhs = rows_k[1, k, :, SHARD * j : SHARD * (j + 1)]
                total += jnp.dot(lhs, up_v[at, :], preferred_element_type=F32)
            return total

        def go(src, dst, send, recv, who):
            copy = pltpu.make_async_remote_copy(
                src_ref=src, dst_ref=dst, send_sem=send, recv_sem=recv, device_id=who, device_id_type=MESH
            )
            copy.start()
            made.append(copy)
            return copy

        far = {}
        for mat in (0, 1):
            ready(mat, 2)
            value = product(mat, 2).astype(BF16)
            for i in (0, 1):
                far_out[mat, i] = value[half * i : half * (i + 1)]
                far[mat, i] = go(
                    far_out.at[mat, i], far_in.at[mat, i], far_s.at[mat, i], far_r.at[mat, i],
                    along(mat, 1 - 2 * i),
                )
        near = []

        def send_near(i, mat, part_i):
            near.append(
                go(
                    near_out.at[i, mat, part_i], near_in.at[i, mat, part_i],
                    near_s.at[i, mat, part_i], near_r.at[i, mat, part_i], along(mat, 1 - 2 * i),
                )
            )

        for i in (0, 1):
            for mat in (0, 1):
                ready(mat, 1 + 2 * i)
                value = product(mat, 1 + 2 * i)
                near_keep[i, mat] = value[half * i : half * (i + 1)]
                near_out[i, mat, 1 - i] = value[half * (1 - i) : half * (2 - i)].astype(BF16)
                send_near(i, mat, 1 - i)
        for i in (0, 1):
            for mat in (0, 1):
                far[mat, i].wait_recv()
                near_out[i, mat, i] = (near_keep[i, mat] + far_in[mat, i].astype(F32)).astype(BF16)
                send_near(i, mat, i)
        for mat in (0, 1):
            ready(mat, 0)
            accs[mat][...] = product(mat, 0)

        def collect():
            for copy in near:
                copy.wait_recv()
            for mat in (0, 1):
                for i in (0, 1):
                    rows = slice(half * i, half * (i + 1))
                    accs[mat][rows, :] += near_in[0, mat, i].astype(F32) + near_in[1, mat, i].astype(F32)

        def finish():
            for copy in made:
                copy.wait_send()

        return collect, finish

    def attended():
        return att[...].reshape(ROWS, HEADS * HEAD_DIM)

    gather_0()
    tables()
    loads["blocks"].wait()
    norm_local()
    res[...] = x_v[pl.ds(my_rows, OWN), :].astype(F32)
    loads["wq"].wait()
    loads["wkv"].wait()
    for name in ("prompt", "cache", "wo", "wd", "tok"):
        loads[name].start()
    project(lambda k: None)
    loads["prompt"].wait()
    loads["cache"].wait()
    attention()
    loads["wo"].wait()
    own, rs_done = reduce_scatter(attended(), wo_v)
    for mat in (0, 1):
        turn(mat, 0)
    after_attention(own, mlp_gain)
    rs_done()
    ready, rows_done = slice_rows(own_onward)
    collect, sums_done = slice_gate_up(ready)
    collect()
    for mat in (0, 1):
        turn(mat, 1)
        spread(mat, -1)
        spread(mat, 1)
    rows_done()
    sums_done()
    activate()
    loads["wd"].wait()
    loads["tok"].wait()
    own, rs_done = reduce_scatter(hid[...], wd_v)
    between_passes(own)
    rs_done()

    ready, ag_done = share_rows()
    project(ready)
    ag_done()
    for mat in (0, 1):
        forward(mat, -1)
        spread(mat, 2)
    attention()
    for mat in (0, 1):
        forward(mat, 1)
    own, rs_done = reduce_scatter(attended(), wo_v)
    after_attention(own, mlp_gain)
    rs_done()
    ready, ag_done = share_rows()
    for mat in (0, 1):
        forward(mat, 2)
    for k in range(N_AG):
        ready(k)
    for dy in (0, -1, 1, 2):
        if dy == 2:
            for a in (0, -1, 1, 2):
                halves(0, a, 2)
        halves(1, dy, 2)
        at = pl.ds(pl.multiple_of(add4(y, dy) * SLICE, SLICE), SLICE)
        for acc, weight in ((g_acc, gate_v), (u_acc, up_v)):
            product = jnp.dot(nrm[:, at], weight[at, :], preferred_element_type=F32)
            if dy == 0:
                acc[...] = product
            else:
                acc[...] += product
    ag_done()
    for copy in sends[0] + sends[1]:
        copy.wait_send()
    activate()
    own, rs_done = reduce_scatter(hid[...], wd_v)
    for n in range(N_RS):
        cols = slice(n * RS_W, (n + 1) * RS_W)
        nrm[pl.ds(my_rows, OWN), cols] = (res[:, cols] + own(n)).astype(BF16)
    rs_done()
    ready, ag_done = share_rows()
    for k in range(N_AG):
        ready(k)
    ag_done()
    copy = pltpu.make_async_copy(nrm, out, load_sem.at[0])
    copy.start()
    copy.wait()


def body(
    blocks, token_embed, accepted, prompt_len, cache_len, prompt_kv, cache_kv, attn_gain,
    w_q, w_kv, w_o, mlp_gain, w_gate, w_up, w_down,
):
    half = np.arange(HEAD_DIM // 2, dtype=np.float32)
    frequency = np.float32(THETA) ** (np.float32(-2.0) * half / np.float32(HEAD_DIM))
    frequency = jnp.asarray(np.concatenate([frequency, frequency])[None, :], dtype=F32)

    vmem = pl.BlockSpec(memory_space=pltpu.VMEM)
    anywhere = pl.BlockSpec(memory_space=pl.ANY)
    dma = pltpu.SemaphoreType.DMA
    return pl.pallas_call(
        kernel,
        out_shape=jax.ShapeDtypeStruct((ROWS, D), BF16),
        in_specs=[pl.BlockSpec(memory_space=pltpu.SMEM)] * 2 + [vmem] * 4 + [anywhere] * 10,
        out_specs=anywhere,
        scratch_shapes=[
            pltpu.VMEM((ROWS, D), BF16),
            pltpu.VMEM((OWN, D), BF16),
            pltpu.VMEM((PMAX, 2 * HEAD_DIM), BF16),
            pltpu.VMEM((REQS, CACHE, 2 * HEAD_DIM), BF16),
            pltpu.VMEM((D, HEADS * HEAD_DIM), BF16),
            pltpu.VMEM((D, 2 * HEAD_DIM), BF16),
            pltpu.VMEM((HEADS * HEAD_DIM, D), BF16),
            pltpu.VMEM((D, HIDDEN), BF16),
            pltpu.VMEM((D, HIDDEN), BF16),
            pltpu.VMEM((HIDDEN, D), BF16),
            pltpu.VMEM((ROWS, D), BF16),
            pltpu.VMEM((ROWS, (HEADS + 2) * HEAD_DIM), F32),
            pltpu.VMEM((REQS, HEADS * BLOCK, HEAD_DIM), BF16),
            pltpu.VMEM((REQS, BLOCK, HEAD_DIM), BF16),
            pltpu.VMEM((REQS, BLOCK, HEAD_DIM), BF16),
            pltpu.VMEM((REQS, BLOCK, HEADS * HEAD_DIM), BF16),
            pltpu.VMEM((ROWS, HIDDEN), F32),
            pltpu.VMEM((ROWS, HIDDEN), F32),
            pltpu.VMEM((ROWS, HIDDEN), BF16),
            pltpu.VMEM((N_RS, ROWS, RS_W), F32),
            pltpu.VMEM((N_RS, 64, RS_W), BF16),
            pltpu.VMEM((N_RS, 64, RS_W), BF16),
            pltpu.VMEM((N_RS, 4, OWN, RS_W), BF16),
            pltpu.VMEM((N_RS, 4, OWN, RS_W), BF16),
            pltpu.VMEM((OWN, D), F32),
            pltpu.VMEM((ROWS, HEAD_DIM), F32),
            pltpu.VMEM((ROWS, HEAD_DIM), F32),
            pltpu.VMEM((4, OWN, SLICE), BF16),
            pltpu.VMEM((2, 4, ROWS, SLICE), BF16),
            pltpu.VMEM((2, 2, ROWS // 2, HIDDEN), BF16),
            pltpu.VMEM((2, 2, ROWS // 2, HIDDEN), BF16),
            pltpu.VMEM((2, 2, ROWS // 2, HIDDEN), F32),
            pltpu.VMEM((2, 2, 2, ROWS // 2, HIDDEN), BF16),
            pltpu.VMEM((2, 2, 2, ROWS // 2, HIDDEN), BF16),
            dma((10,)),
            dma((2, 20)),
            dma((2, 4, 4, 2)),
            dma((N_RS,)),
            dma((N_RS,)),
            dma((N_RS, 4)),
            dma((N_RS, 4)),
            dma((N_AG, 4)),
            dma((N_AG, 4)),
            dma((N_AG, 4)),
            dma((N_AG, 4)),
            dma((2, 4)),
            dma((2, 4)),
            dma((2, 4, 4)),
            dma((2, 4, 4)),
            dma((2, 4, 4)),
            dma((2, 4, 4)),
            dma((2, 2)),
            dma((2, 2)),
            dma((2, 2, 2)),
            dma((2, 2, 2)),
        ],
        compiler_params=pltpu.CompilerParams(
            collective_id=0, has_side_effects=True, vmem_limit_bytes=60 * 2**20
        ),
        name="two_passes",
    )(
        prompt_len[None, :], cache_len, accepted[None, :], frequency, attn_gain[None, :], mlp_gain[None, :],
        blocks, token_embed, prompt_kv[0], cache_kv[0], w_q, w_kv, w_o, w_gate, w_up, w_down,
    )


def solution(mesh):
    return jax.shard_map(
        body,
        mesh=mesh,
        in_specs=(
            P("req", None),
            P("req", None),
            P("req"),
            P("req"),
            P("req", None),
            P("req", None, "mlp"),
            P("req", None, None, "mlp"),
            P(),
            P(None, "mlp"),
            P(None, "mlp"),
            P("mlp", None),
            P(),
            P("req", "mlp"),
            P("req", "mlp"),
            P("mlp", None),
        ),
        out_specs=P("req", None),
        check_vma=False,
    )
```
